128 devices in a mesh: gx: 16 (over z, y), gy: 8 (over x, core).
Axes of the slice: x: 4, y: 4, z: 4, core: 2. Of those that a mesh axis runs over, the one named last changes fastest.
Arguments:
- ocean_temp: float32 [64, 64, 2048], P(None, 'gy', 'gx'), may hold values from -2 to 1.5
- ocean_salt: float32 [64, 64, 2048], P(None, 'gy', 'gx'), may hold values from 33.8 to 34.8
- wet_mask: int32 [64, 64, 2048], P(None, 'gy', 'gx'), may hold values 0 or 1
- vertical_mix: float32 [64, 2048], P('gy', 'gx'), may hold values from 0.05 to 0.3
- friction: float32 [64, 2048], P('gy', 'gx'), may hold values from 0.5 to 5
- pressure: float32 [64, 2048], P('gy', 'gx'), may hold values from 200 to 1500
- pair_column: int32 [65536, 128], P(('gx', 'gy')), may hold values from 0 to 1023
- pair_weight: float32 [65536, 128], P(('gx', 'gy')), may hold values from 0.05 to 1
- block_owner: int32 [65536, 1], P(('gx', 'gy')), may hold values from 0 to 127; in each aligned block of 512 rows (0 to 511, 512 to 1023, ...) at most 8 rows name the same one
- block_target: int32 [65536], P(('gx', 'gy')), may hold values from 0 to 31
- enthalpy: float32 [40, 524288], P(None, ('gx', 'gy')), may hold values from -1 to 0.2
- surface_enthalpy: float32 [524288], P(('gx', 'gy')), may hold values from -1.5 to -0.5
- transition_layer: int32 [524288], P(('gx', 'gy')), may hold values from 0 to 40
- column_area: float32 [524288], P(('gx', 'gy')), may hold values from 0.5 to 2
Outputs:
- new_temp: float32 [64, 64, 2048], P(None, 'gy', 'gx')
- new_salt: float32 [64, 64, 2048], P(None, 'gy', 'gx')
- new_enthalpy: float32 [40, 524288], P(None, ('gx', 'gy'))
- ice_melt: float32 [524288], P(('gx', 'gy'))
The draws below stay inside these ranges and needn't reach their ends.
Inputs may be any that keep to these rules, and one draw needn't show every extreme that they name: `block_owner`: of the 512 blocks of one device at most 8 name the same owner, and some owner gets exactly 8 of them.
All inputs are finite; a program needn't handle non-finite values. No bound on the sum of `wet_mask` on one device may be relied on, other than what follows from the above.
Results may differ from the reference program's by a relative error of at most 0.000059.
Values sent between devices are 32-bit elements; how exact they have to be, the bound alone decides.
No kernel may reach another device: no remote copies, remote signals or barrier semaphores. Data moves between devices by JAX's collectives and lax.ppermute only.
A program may use at most 64 MiB of HBM per device.

```python
import math
import jax
import jax.numpy as jnp
import numpy as np
from jax import lax

KL = 64
NL = 40
BW = 128
CJ = 8
CI = 128
NBLK = 512
ICEBLK = 32
CAP = 8
NJ = 64
NI = 2048
IC_DEV = 4096
ICE = 524288
BLOCKS = 65536
N_GY = 8
DEVICES = 128


def touch_ends(values, own_key, smallest, largest):
    shape = values.shape
    place = [jax.random.randint(jax.random.fold_in(own_key, axis), (), 0, shape[axis]) for axis in range(len(shape))]
    values = values.at[tuple(place)].set(smallest)
    longest = shape.index(max(shape))
    place[longest] = (place[longest] + 1) % shape[longest]
    return values.at[tuple(place)].set(largest)


def level_of(own_key, dims, pieces, low, high):
    factor_of, own = 1.0, jax.random.fold_in(own_key, 6)
    for axis_at, shards_of in pieces:
        draws = jnp.exp(jax.random.uniform(jax.random.fold_in(own, axis_at), (shards_of,), jnp.float32, low / len(pieces), high / len(pieces)))
        factor_of = factor_of * jnp.repeat(draws, dims[axis_at] // shards_of).reshape([-1 if axis == axis_at else 1 for axis in range(len(dims))])
    return factor_of


def deal_out(rng, own, number, rows, number_of, top, most, slope):
    order = jax.random.permutation(rng, number_of)
    crowded, common = shares(number_of, rows * top, most, slope, True), shares(number_of, rows * top, most, slope, False)
    places = jnp.arange(number_of)

    def named(lengths, turn):
        used = int((lengths > 0).sum())
        fixed = max(1, used // 4)
        shifted = fixed + (places - fixed + turn * (used - fixed)) % max(1, number_of - fixed)
        return jnp.zeros((number_of,), jnp.int32).at[order[jnp.where(places < fixed, places, shifted)]].set(jnp.asarray(lengths, jnp.int32))

    lengths = jnp.where(number % 4 == 0, named(crowded, number // 4), named(common, number - number // 4 - 1))
    mixed = jax.random.permutation(jax.random.fold_in(own, 3), number_of)
    giver, taker = mixed[0:number_of // 2 * 2:2], mixed[1:number_of // 2 * 2:2]
    margin = jnp.minimum(lengths[giver] - 1, most - lengths[taker]) // 2
    margin = jnp.where((giver == order[0]) | (taker == order[0]) | (lengths[taker] == 0), 0, jnp.maximum(margin, 0))
    shifted = jax.random.randint(jax.random.fold_in(own, 4), (number_of // 2,), 0, 1 << 20) % (margin + 1)
    lengths = lengths.at[giver].add(-shifted).at[taker].add(shifted)
    members = jnp.searchsorted(jnp.cumsum(lengths), jnp.arange(rows * top), side="right").astype(jnp.int32)
    grid = members.reshape(top, rows).T
    grid = grid[jax.random.permutation(jax.random.fold_in(own, 1), rows)]
    turn = jax.random.randint(jax.random.fold_in(own, 2), (rows, 1), 0, top)
    return jnp.take_along_axis(grid, (jnp.arange(top)[None, :] + turn) % top, axis=1)


def shares(count, total, reach, skew, full):
    weights = [(1 << 20) // math.isqrt(rank ** skew) + 1 for rank in range(1, count + 1)]
    largest = reach if full else min(reach, max(-(-total // count), total * weights[0] // sum(weights)))
    least = 1 if total - largest >= count - 1 else 0
    holding, surplus = [largest] + [least] * (count - 1), total - largest - least * (count - 1)
    while surplus > 0:
        candidates = [i for i in range(1, count) if holding[i] < largest] or [i for i in range(1, count) if holding[i] < reach]
        whole, remaining = sum([weights[i] for i in candidates]), surplus
        for i in candidates:
            more = min(reach - holding[i], max(1, remaining * weights[i] // whole), surplus)
            holding[i] = holding[i] + more
            surplus = surplus - more
    return np.array(holding)


def setup_inputs(seed: int = 0) -> dict:
    keys = jax.random.split(jax.random.key(seed), 15)
    ocean_temp = jnp.clip(-2.0 + 3.5 * jax.random.uniform(keys[0], (KL, NJ, NI), jnp.float32) ** level_of(keys[0], (KL, NJ, NI), ((1, 8), (2, 16)), -0.2, 0.2), -2.0, 1.5)
    ocean_salt = jnp.clip(33.8 + 1.0 * jax.random.uniform(keys[1], (KL, NJ, NI), jnp.float32) ** level_of(keys[1], (KL, NJ, NI), ((1, 8), (2, 16)), -0.2, 0.2), 33.8, 34.8)
    wet_mask = touch_ends((jax.random.randint(keys[2], (KL, NJ, NI), 0, 8) < 7).astype(jnp.int32), jax.random.fold_in(keys[2], 1), 0, 1)
    vertical_mix = jnp.clip(0.05 + 0.25 * jax.random.uniform(keys[3], (NJ, NI), jnp.float32) ** level_of(keys[3], (NJ, NI), ((0, 8), (1, 16)), -0.2, 0.2), 0.05, 0.3)
    friction = jnp.clip(jnp.exp(math.log(5.0) - 2.3025851 * jax.random.uniform(keys[4], (NJ, NI), jnp.float32) ** level_of(keys[4], (NJ, NI), ((0, 8), (1, 16)), -0.2, 0.2)), 0.5, 5.0)
    pressure = jnp.clip(200.0 + 1300.0 * jax.random.uniform(keys[5], (NJ, NI), jnp.float32) ** level_of(keys[5], (NJ, NI), ((0, 8), (1, 16)), -0.2, 0.2), 200.0, 1500.0)
    pair_column = touch_ends(jax.random.randint(keys[6], (BLOCKS, BW), 0, CJ * CI), jax.random.fold_in(keys[6], 1), 0, (CJ * CI) - 1).astype(jnp.int32)
    pair_weight = jnp.clip(jnp.exp(math.log(1.0) - 2.9957323 * jax.random.uniform(keys[7], (BLOCKS, BW), jnp.float32) ** level_of(keys[7], (BLOCKS, BW), ((0, 128),), -0.2, 0.2)), 0.05, 1.0)
    block_owner_keys = jax.random.split(jax.random.fold_in(keys[8], 1), BLOCKS // NBLK)
    block_owner_turns = jax.random.permutation(jax.random.fold_in(keys[8], 3), BLOCKS // NBLK)
    block_owner = jax.vmap(lambda own, number: deal_out(jax.random.fold_in(keys[8], 2), own, number, NBLK, DEVICES, 1, CAP, 2))(block_owner_keys, block_owner_turns).reshape((BLOCKS, 1))
    block_target = touch_ends(jax.random.randint(keys[9], (BLOCKS,), 0, ICEBLK), jax.random.fold_in(keys[9], 1), 0, ICEBLK - 1).astype(jnp.int32)
    enthalpy = jnp.clip(-1.0 + 1.2 * jax.random.uniform(keys[10], (NL, ICE), jnp.float32) ** level_of(keys[10], (NL, ICE), ((1, 128),), -0.2, 0.2), -1.0, 0.2)
    surface_enthalpy = jnp.clip(-1.5 + 1.0 * jax.random.uniform(keys[11], (ICE,), jnp.float32) ** level_of(keys[11], (ICE,), ((0, 128),), -0.2, 0.2), -1.5, -0.5)
    transition_layer = touch_ends(jax.random.randint(keys[12], (ICE,), 0, NL + 1), jax.random.fold_in(keys[12], 1), 0, NL).astype(jnp.int32)
    column_area = jnp.clip(jnp.exp(math.log(2.0) - 1.3862944 * jax.random.uniform(keys[13], (ICE,), jnp.float32) ** level_of(keys[13], (ICE,), ((0, 128),), -0.2, 0.2)), 0.5, 2.0)
    return dict(ocean_temp=ocean_temp, ocean_salt=ocean_salt, wet_mask=wet_mask, vertical_mix=vertical_mix, friction=friction, pressure=pressure, pair_column=pair_column, pair_weight=pair_weight, block_owner=block_owner, block_target=block_target, enthalpy=enthalpy, surface_enthalpy=surface_enthalpy, transition_layer=transition_layer, column_area=column_area)


mixing_rate = 0.2
liquidus_slope = -0.0573
liquidus_base = 0.0832
liquidus_depth = -0.000753
latent_ratio = 4.0
salt_ratio = 35.0
relax_rate = 0.1
cold_rate = 2.0
temperate_rate = 0.2

def spread_sideways(extended, wet_ext):
    middle = extended[:, :, 1:-1, 1:-1]
    wet_mid = wet_ext[:, 1:-1, 1:-1]
    height = middle.shape[2]
    breadth = middle.shape[3]
    change = jnp.zeros_like(middle)
    for row_off, col_off in ((0, 1), (2, 1), (1, 0), (1, 2)):
        beside = extended[:, :, row_off:row_off + height, col_off:col_off + breadth]
        wet_beside = wet_ext[:, row_off:row_off + height, col_off:col_off + breadth]
        change = change + (wet_mid * wet_beside)[None] * (beside - middle)
    return middle + mixing_rate * change

def mix_vertical(fields, wetness, vertical_mix):
    link = wetness[:-1] * wetness[1:]
    level_flux = vertical_mix[None, None] * link[None] * (fields[:, 1:] - fields[:, :-1])
    return fields + jnp.pad(level_flux, ((0, 0), (0, 1), (0, 0), (0, 0))) - jnp.pad(level_flux, ((0, 0), (1, 0), (0, 0), (0, 0)))

def shelf_melt(surface_temp, surface_salt, friction, pressure, wet_top):
    heat_gain = jnp.where(wet_top > 0, friction, 1.0)
    salt_safe = jnp.where(wet_top > 0, surface_salt, 34.0)
    salt_gain = heat_gain / salt_ratio
    curvature = heat_gain * liquidus_slope
    linear = heat_gain * (surface_temp - liquidus_base - liquidus_depth * pressure) + latent_ratio * salt_gain
    constant = latent_ratio * salt_gain * salt_safe
    boundary_salt = 2.0 * constant / (linear + jnp.sqrt(linear * linear - 4.0 * curvature * constant))
    boundary_temp = liquidus_slope * boundary_salt + liquidus_base + liquidus_depth * pressure
    heat_flux = heat_gain * (surface_temp - boundary_temp) * wet_top
    salt_flux = salt_gain * (salt_safe - boundary_salt) * wet_top
    return (heat_flux, salt_flux, boundary_temp * wet_top)

def ocean_update(extended, wet_ext, vertical_mix, friction, pressure):
    fields = spread_sideways(extended, wet_ext)
    wetness = wet_ext[:, 1:-1, 1:-1]
    fields = mix_vertical(fields, wetness, vertical_mix)
    heat_flux, salt_flux, base_temp = shelf_melt(fields[0, 0], fields[1, 0], friction, pressure, wetness[0])
    top_level = jnp.stack([fields[0, 0] - relax_rate * heat_flux, fields[1, 0] - relax_rate * salt_flux])
    fields = fields.at[:, 0].set(top_level)
    return (fields, heat_flux / latent_ratio, base_temp)

def solve_columns(enthalpy, transition_layer, surface_enthalpy, cover_sum, base_sum):
    layers = enthalpy.shape[0]
    level = jnp.arange(layers, dtype=jnp.int32)[:, None]
    rate = jnp.where(level < transition_layer[None, :], cold_rate, temperate_rate).astype(jnp.float32)
    inner = 0.5 * (rate[:-1] + rate[1:])
    zero_row = jnp.zeros_like(rate[:1])
    lower = jnp.concatenate([rate[:1], inner], axis=0)
    upper = jnp.concatenate([inner, cover_sum[None, :]], axis=0)
    diagonal = 1.0 + lower + upper
    below = -jnp.concatenate([zero_row, inner], axis=0)
    above = -jnp.concatenate([inner, zero_row], axis=0)
    right_side = enthalpy.at[0].add(rate[0] * surface_enthalpy).at[layers - 1].add(base_sum)

    def forward(carry, items):
        ratio_prev, value_prev = carry
        diag_now, below_now, above_now, side_now = items
        pivot = diag_now - below_now * ratio_prev
        ratio_now = above_now / pivot
        value_now = (side_now - below_now * value_prev) / pivot
        return ((ratio_now, value_now), (ratio_now, value_now))
    start = (jnp.zeros_like(rate[0]), jnp.zeros_like(rate[0]))
    unused, (ratios, values) = lax.scan(forward, start, (diagonal, below, above, right_side))

    def backward(next_value, items):
        ratio_now, value_now = items
        result = value_now - ratio_now * next_value
        return (result, result)
    unused_last, solved = lax.scan(backward, jnp.zeros_like(rate[0]), (ratios, values), reverse=True)
    return solved

def reference(ocean_temp, ocean_salt, wet_mask, vertical_mix, friction, pressure, pair_column, pair_weight, block_owner, block_target, enthalpy, surface_enthalpy, transition_layer, column_area):
    wetness = wet_mask.astype(jnp.float32)
    wet_ext = jnp.pad(wetness, ((0, 0), (1, 1), (1, 1)))
    fields = jnp.stack([ocean_temp, ocean_salt])
    melt_total = jnp.zeros_like(friction)
    base_total = jnp.zeros_like(friction)
    for step in range(2):
        extended = jnp.pad(fields, ((0, 0), (0, 0), (1, 1), (1, 1)))
        fields, melt_rate, base_temp = ocean_update(extended, wet_ext, vertical_mix, friction, pressure)
        melt_total = melt_total + melt_rate
        base_total = base_total + base_temp
    mean_melt = (0.5 * melt_total).reshape(-1)
    mean_base = (0.5 * base_total).reshape(-1)
    device = jnp.arange(BLOCKS, dtype=jnp.int32) // NBLK
    tile_col = device // N_GY
    tile_row = device % N_GY
    cell_row = pair_column // CI
    cell_col = pair_column % CI
    ocean_index = (tile_row[:, None] * CJ + cell_row) * NI + tile_col[:, None] * CI + cell_col
    ice_index = block_owner[:, 0][:, None] * IC_DEV + block_target[:, None] * BW + jnp.arange(BW, dtype=jnp.int32)[None, :]
    flat_ice = ice_index.reshape(-1)
    melt_terms = (pair_weight * mean_melt[ocean_index]).reshape(-1)
    base_terms = (pair_weight * mean_base[ocean_index]).reshape(-1)
    melt_sum = jax.ops.segment_sum(melt_terms, flat_ice, num_segments=ICE) / column_area
    base_sum = jax.ops.segment_sum(base_terms, flat_ice, num_segments=ICE) / column_area
    cover_sum = jax.ops.segment_sum(pair_weight.reshape(-1), flat_ice, num_segments=ICE) / column_area
    new_enthalpy = solve_columns(enthalpy, transition_layer, surface_enthalpy, cover_sum, base_sum)
    return (fields[0], fields[1], new_enthalpy, melt_sum)
```

```python
import jax
import jax.numpy as jnp
from jax import lax
from jax.experimental import pallas as pl
from jax.experimental.pallas import tpu as pltpu
from jax.sharding import PartitionSpec as P

mixing_rate = 0.2
liquidus_slope = -0.0573
liquidus_base = 0.0832
liquidus_depth = -0.000753
latent_ratio = 4.0
salt_ratio = 35.0
relax_rate = 0.1
cold_rate = 2.0
temperate_rate = 0.2

f32 = jnp.float32
bf16 = jnp.bfloat16
levels = 64
slots = 8
chunk = 3 * slots + 1
halo_rows = 392


def lanes_of(shape):
    return lax.broadcasted_iota(jnp.int32, shape, len(shape) - 1)


def call(body, outs, ins, in_specs=None, scratch=(), cost=(0, 0)):
    return pl.pallas_call(
        body,
        out_shape=outs,
        grid=(1,),
        in_specs=in_specs,
        out_specs=jax.tree.map(lambda o: whole(o.shape), outs),
        scratch_shapes=scratch,
        cost_estimate=pl.CostEstimate(flops=cost[0], bytes_accessed=cost[1], transcendentals=0),
    )(*ins)


def whole(shape):
    return pl.BlockSpec(tuple(shape), lambda i: (0,) * len(shape))


def part(shape, *index):
    return pl.BlockSpec(tuple(shape), lambda i: index)


def row_pack_body(temp, salt, wet, mix, friction, pressure, up, down):
    for k in range(levels):
        for field, source in enumerate((temp, salt, wet)):
            at = 2 * (field * levels + k)
            up[at : at + 2, :] = source[k, 0:2, :].astype(f32)
            down[at : at + 2, :] = source[k, 6:8, :].astype(f32)
    for place, source in enumerate((mix, friction, pressure)):
        at = 2 * (3 * levels + place)
        up[at : at + 2, :] = source[0:2, :]
        down[at : at + 2, :] = source[6:8, :]
    up[390:392, :] = jnp.zeros((2, 128), f32)
    down[390:392, :] = jnp.zeros((2, 128), f32)


def col_pack_body(temp, salt, wet, mix, friction, pressure, top, bottom, left, right, tall):
    zeros = jnp.zeros((8, 128), f32)
    half = lanes_of((16, 128)) // 2

    def plane(at, centre):
        tall[at, 0:8, :] = centre
        tall[at, 8:16, :] = zeros
        tall[at, 8:10, :] = bottom[2 * at : 2 * at + 2, :]
        tall[at, 14:16, :] = top[2 * at : 2 * at + 2, :]

    for field, source in enumerate((temp, salt, wet)):
        for k in range(levels):
            plane(field * levels + k, source[k].astype(f32))
    for place, source in enumerate((mix, friction, pressure)):
        plane(3 * levels + place, source[...])
    for group in range(4):
        count = levels if group < 3 else 3
        go_left = jnp.zeros((16, 128), f32)
        go_right = jnp.zeros((16, 128), f32)
        for k in range(count):
            value = tall[group * levels + k]
            here = half == k
            go_left = jnp.where(here, pltpu.roll(value, 2 * k, 1), go_left)
            go_right = jnp.where(here, pltpu.roll(value, (2 * k + 2) % 128, 1), go_right)
        left[16 * group : 16 * group + 16, :] = go_left
        right[16 * group : 16 * group + 16, :] = go_right


def sides_of(from_right, from_left, back, ahead):
    lane = lanes_of((16, 128))
    return jnp.where(
        lane < 64, pltpu.roll(from_right, back, 1), pltpu.roll(from_left, ahead, 1)
    )


def dry_gap(side):
    lane = lanes_of((16, 128))
    return jnp.where((lane < 2) | (lane >= 126), side, 0.0)


def beside(value):
    rows, cols = value.shape
    return (
        pltpu.roll(value, 1, 0),
        pltpu.roll(value, rows - 1, 0),
        pltpu.roll(value, 1, 1),
        pltpu.roll(value, cols - 1, 1),
    )


def spread(value, links):
    change = jnp.zeros_like(value)
    for link, near in zip(links, beside(value)):
        change = change + link * (near - value)
    return value + mixing_rate * change


def links_of(wet):
    return tuple(wet * near for near in beside(wet))


def shelf_melt(surface_temp, surface_salt, friction, pressure, wet_top):
    heat_gain = jnp.where(wet_top > 0, friction, 1.0)
    salt_safe = jnp.where(wet_top > 0, surface_salt, 34.0)
    salt_gain = heat_gain / salt_ratio
    curvature = heat_gain * liquidus_slope
    linear = (
        heat_gain * (surface_temp - liquidus_base - liquidus_depth * pressure)
        + latent_ratio * salt_gain
    )
    constant = latent_ratio * salt_gain * salt_safe
    boundary_salt = (
        2.0 * constant / (linear + jnp.sqrt(linear * linear - 4.0 * curvature * constant))
    )
    boundary_temp = liquidus_slope * boundary_salt + liquidus_base + liquidus_depth * pressure
    heat_flux = heat_gain * (surface_temp - boundary_temp) * wet_top
    salt_flux = salt_gain * (salt_safe - boundary_salt) * wet_top
    return heat_flux, salt_flux, boundary_temp * wet_top


def centre_of(value):
    return value[0:8, 0:128]


def surface_body(
    temp,
    salt,
    wet,
    mix,
    friction,
    pressure,
    top_temp,
    top_salt,
    top_wet,
    top_rest,
    low_temp,
    low_salt,
    low_wet,
    low_rest,
    from_right,
    from_left,
    slot_row,
    slot_lane,
    slot_weight,
    slot_target,
    send,
    tall,
):
    def plane(at, group, k, centre, top, bottom, offset):
        tall[at, 0:8, 0:128] = centre
        tall[at, 8:16, 0:128] = jnp.zeros((8, 128), f32)
        tall[at, 8:10, 0:128] = bottom[offset : offset + 2, :]
        tall[at, 14:16, 0:128] = top[offset : offset + 2, :]
        side = sides_of(
            from_right[16 * group : 16 * group + 16, :],
            from_left[16 * group : 16 * group + 16, :],
            (128 - 2 * k) % 128,
            126 - 2 * k,
        )
        tall[at, :, 128:256] = dry_gap(side) if group == 2 else side

    for k in range(3):
        plane(k, 0, k, temp[k], top_temp, low_temp, 2 * k)
        plane(3 + k, 1, k, salt[k], top_salt, low_salt, 2 * k)
        plane(6 + k, 2, k, wet[k].astype(f32), top_wet, low_wet, 2 * k)
    for place, (source) in enumerate((mix, friction, pressure)):
        plane(9 + place, 3, place, source[...], top_rest, low_rest, 2 * place)

    wets = [tall[6 + k] for k in range(3)]
    mixing = tall[9]
    rub = tall[10]
    press = tall[11]
    first = mixing * (wets[0] * wets[1])
    second = mixing * (wets[1] * wets[2])
    links = [links_of(value) for value in wets]
    stepped = []
    for field in range(2):
        near = [spread(tall[3 * field + k], links[k]) for k in range(3)]
        flux = first * (near[1] - near[0])
        under = second * (near[2] - near[1])
        stepped.append((near[0] + flux, near[1] + under - flux))
    heat, brine, base_one = shelf_melt(stepped[0][0], stepped[1][0], rub, press, wets[0])
    tops = (stepped[0][0] - relax_rate * heat, stepped[1][0] - relax_rate * brine)
    later = []
    for field in range(2):
        near0 = spread(tops[field], links[0])
        near1 = spread(stepped[field][1], links[1])
        later.append(centre_of(near0 + first * (near1 - near0)))
    heat_two, unused, base_two = shelf_melt(
        later[0], later[1], friction[...], pressure[...], centre_of(wets[0])
    )
    melt = 0.5 * (centre_of(heat) / latent_ratio + heat_two / latent_ratio)
    base = 0.5 * (centre_of(base_one) + base_two)

    melts = [jnp.broadcast_to(melt[r : r + 1, :], (8, 128)) for r in range(8)]
    bases = [jnp.broadcast_to(base[r : r + 1, :], (8, 128)) for r in range(8)]

    def owners(i, carry):
        out = send.at[pl.ds(pl.multiple_of(8 * chunk * i, 8), 8 * chunk)]
        for j in range(8):
            at = pl.ds(pl.multiple_of(64 * i + 8 * j, 8), 8)
            lane = slot_lane[at, :]
            row = slot_row[at, :]
            weight = slot_weight[at, :]
            melt_here = jnp.take_along_axis(melts[0], lane, axis=1)
            base_here = jnp.take_along_axis(bases[0], lane, axis=1)
            for r in range(1, 8):
                hit = row == r
                melt_here = jnp.where(
                    hit, jnp.take_along_axis(melts[r], lane, axis=1), melt_here
                )
                base_here = jnp.where(
                    hit, jnp.take_along_axis(bases[r], lane, axis=1), base_here
                )
            out[chunk * j : chunk * j + 8, :] = weight * melt_here
            out[chunk * j + 8 : chunk * j + 16, :] = weight * base_here
            out[chunk * j + 16 : chunk * j + 24, :] = weight
        targets = slot_target[pl.ds(pl.multiple_of(8 * i, 8), 8), :]
        for j in range(8):
            out[chunk * j + 24 : chunk * j + 25, :] = targets[j : j + 1, :]
        return carry

    lax.fori_loop(0, 16, owners, 0)


def slot_body(owner, target, column, weight, slot_row, slot_lane, slot_weight, slot_target):
    count = owner.shape[0]
    across = jnp.broadcast_to(owner[...], (count, count))
    row = lax.broadcasted_iota(jnp.int32, (count, count), 0)
    col = lax.broadcasted_iota(jnp.int32, (count, count), 1)
    same = row == col
    owner_lane = jnp.sum(jnp.where(same, across, 0), axis=0, keepdims=True)
    alike = across == owner_lane
    rank_lane = jnp.sum(jnp.where(alike & (row < col), 1, 0), axis=0, keepdims=True)
    rank_row = jnp.sum(jnp.where(alike & (col < row), 1, 0), axis=1, keepdims=True)
    target_row = jnp.sum(jnp.where(same, target[...], 0), axis=1, keepdims=True)
    slot = owner_lane * slots + rank_lane
    total = slot_row.shape[0]
    pick = jnp.where(lax.broadcasted_iota(jnp.int32, (total, count), 0) == slot, 1.0, 0.0)
    value = weight[...]
    high = value.astype(bf16)
    rest = value - high.astype(f32)
    middle = rest.astype(bf16)
    low = (rest - middle.astype(f32)).astype(bf16)
    places = column[...]
    table = jnp.concatenate(
        [
            high,
            middle,
            low,
            (places // 128).astype(f32).astype(bf16),
            (places % 128).astype(f32).astype(bf16),
        ],
        axis=1,
    )
    sorted_ = jnp.dot(pick.astype(bf16), table, preferred_element_type=f32)
    slot_weight[...] = sorted_[:, 0:128] + sorted_[:, 128:256] + sorted_[:, 256:384]
    slot_row[...] = sorted_[:, 384:512].astype(jnp.int32)
    slot_lane[...] = sorted_[:, 512:640].astype(jnp.int32)
    lane = lax.broadcasted_iota(jnp.int32, (count, 128), 1)
    spot = jnp.where(rank_row == lane % slots, target_row, 0).astype(f32).astype(bf16)
    holds = jnp.where(lax.broadcasted_iota(jnp.int32, (128, count), 0) == owner_lane, 1.0, 0.0)
    slot_target[...] = jnp.dot(holds.astype(bf16), spot, preferred_element_type=f32)


def ocean_body(
    temp,
    salt,
    wet,
    mix,
    friction,
    pressure,
    top,
    bottom,
    from_right,
    from_left,
    new_temp,
    new_salt,
    tall,
    above,
):
    zeros = jnp.zeros((8, 128), f32)

    def rest_plane(at, source):
        tall[at, 0:8, 0:128] = source[...]
        tall[at, 8:16, 0:128] = zeros
        tall[at, 8:10, 0:128] = bottom[384 + 2 * at : 386 + 2 * at, :]
        tall[at, 14:16, 0:128] = top[384 + 2 * at : 386 + 2 * at, :]
        tall[at, :, 128:256] = sides_of(
            from_right[48:64, :], from_left[48:64, :], (128 - 2 * at) % 128, 126 - 2 * at
        )

    for at, source in enumerate((mix, friction, pressure)):
        rest_plane(at, source)
    mixing = tall[0]

    def build(spot, group, k, centre):
        offset = 2 * (group * levels + k)
        tall[spot, 0:8, 0:128] = centre
        tall[spot, 8:16, 0:128] = zeros
        tall[spot, 8:10, 0:128] = bottom[pl.ds(offset, 2), :]
        tall[spot, 14:16, 0:128] = top[pl.ds(offset, 2), :]
        side = sides_of(
            from_right[16 * group : 16 * group + 16, :],
            from_left[16 * group : 16 * group + 16, :],
            lax.rem(128 - 2 * k, 128),
            126 - 2 * k,
        )
        tall[spot, :, 128:256] = dry_gap(side) if group == 2 else side

    def load(k):
        build(3, 0, k, temp[k])
        build(4, 1, k, salt[k])
        build(5, 2, k, wet[k].astype(f32))
        water = tall[5]
        links = links_of(water)
        near = tuple(spread(tall[3 + field], links) for field in range(2))
        return water, links, near

    def second_step(k, once, water, links, state):
        middle_links = tuple(centre_of(link) for link in links)
        here = []
        for field in range(2):
            change = jnp.zeros((8, 128), f32)
            middle = centre_of(once[field])
            for link, near in zip(middle_links, beside(once[field])):
                change = change + link * (centre_of(near) - middle)
            here.append(middle + mixing_rate * change)
        water_c = centre_of(water)
        return tuple(here), water_c

    def emit(k, field, value):
        (new_temp, new_salt)[field][k] = value

    water0, links0, near0 = load(0)
    water1, links1, near1 = load(1)
    coef = mixing * (water0 * water1)
    flux = tuple(coef * (near1[f] - near0[f]) for f in range(2))
    first = tuple(near0[f] + flux[f] for f in range(2))
    heat, brine, unused = shelf_melt(first[0], first[1], tall[1], tall[2], water0)
    first = (first[0] - relax_rate * heat, first[1] - relax_rate * brine)
    here, water_c = second_step(0, first, water0, links0, None)
    mixing_c = mix[...]
    no_flux = (jnp.zeros((8, 128), f32), jnp.zeros((8, 128), f32))

    def finish(k, here, next_here, water_c, next_water, flux_c):
        coef_c = mixing_c * (water_c * next_water)
        out_flux = tuple(coef_c * (next_here[f] - here[f]) for f in range(2))
        return out_flux

    def advance(k, carry):
        water, links, near, flux, here, water_c, flux_c = carry
        next_water, next_links, next_near = load(k + 1)
        coef = mixing * (water * next_water)
        next_flux = tuple(coef * (next_near[f] - near[f]) for f in range(2))
        once = tuple(near[f] + next_flux[f] - flux[f] for f in range(2))
        next_here, next_c = second_step(k, once, water, links, None)
        out_flux = finish(k - 1, here, next_here, water_c, next_c, flux_c)
        for f in range(2):
            above[f, k - 1] = here[f] + out_flux[f] - flux_c[f]
        return next_water, next_links, next_near, next_flux, next_here, next_c, out_flux

    carry = (water1, links1, near1, flux, here, water_c, no_flux)
    carry = lax.fori_loop(1, levels - 1, advance, carry)
    water, links, near, flux, here, water_c, flux_c = carry
    once = tuple(near[f] - flux[f] for f in range(2))
    next_here, next_c = second_step(levels - 1, once, water, links, None)
    out_flux = finish(levels - 2, here, next_here, water_c, next_c, flux_c)
    for f in range(2):
        above[f, levels - 2] = here[f] + out_flux[f] - flux_c[f]
        above[f, levels - 1] = next_here[f] - out_flux[f]
    heat, brine, unused = shelf_melt(
        above[0, 0], above[1, 0], friction[...], pressure[...], wet[0].astype(f32)
    )
    above[0, 0] = above[0, 0] - relax_rate * heat
    above[1, 0] = above[1, 0] - relax_rate * brine
    new_temp[...] = above[0]
    new_salt[...] = above[1]


def column_body(enthalpy, surface, transition, offset, factor, pivot_end, side_end):
    count = enthalpy.shape[0]
    side = enthalpy[...].reshape(count, 32, 128)
    change_at = transition[...]
    rates = [jnp.where(k < change_at, cold_rate, temperate_rate) for k in range(count)]
    inner = [0.5 * (rates[k] + rates[k + 1]) for k in range(count - 1)]
    ratios = []
    values = []
    for k in range(count - 1):
        if k == 0:
            pivot = 1.0 + rates[0] + inner[0]
            right = side[0] + rates[0] * surface[...]
        else:
            pivot = 1.0 + inner[k - 1] + inner[k] + inner[k - 1] * ratios[-1]
            right = side[k] + inner[k - 1] * values[-1]
        scale = 1.0 / pivot
        ratios.append(-inner[k] * scale)
        values.append(right * scale)
    pivot_end[...] = 1.0 + inner[-1] + inner[-1] * ratios[-1]
    side_end[...] = side[count - 1] + inner[-1] * values[-1]
    offsets = [jnp.zeros((32, 128), f32)]
    factors = [jnp.ones((32, 128), f32)]
    for k in range(count - 2, -1, -1):
        offsets.append(values[k] - ratios[k] * offsets[-1])
        factors.append(-ratios[k] * factors[-1])
    offset[...] = jnp.stack(offsets[::-1]).reshape(count, 4096)
    factor[...] = jnp.stack(factors[::-1]).reshape(count, 4096)


def collect_body(got, area, offset, factor, pivot_end, side_end, new_enthalpy, melt):
    sums = jnp.zeros((32, 384), f32)
    lane = lax.broadcasted_iota(jnp.int32, (1, 128), 1) // slots
    wanted = lax.broadcasted_iota(jnp.int32, (32, 128), 0).astype(f32)
    for group in range(8):
        parts = ([], [], [])
        target = jnp.zeros((1, 128), f32)
        for s in range(16):
            at = chunk * (16 * group + s)
            for place in range(3):
                parts[place].append(got[at + 8 * place : at + 8 * place + 8, :])
            target = jnp.where(lane == s, got[at + 24 : at + 25, :], target)
        hot = jnp.where(wanted == target, 1.0, 0.0).astype(bf16)
        value = jnp.concatenate([jnp.concatenate(p, axis=0) for p in parts], axis=1)
        high = value.astype(bf16)
        rest = value - high.astype(f32)
        middle = rest.astype(bf16)
        low = (rest - middle.astype(f32)).astype(bf16)
        for piece in (high, middle, low):
            sums = sums + jnp.dot(hot, piece, preferred_element_type=f32)
    size = area[...]
    melt[...] = sums[:, 0:128] / size
    base_sum = sums[:, 128:256] / size
    cover_sum = sums[:, 256:384] / size
    last = (side_end[...] + base_sum) / (pivot_end[...] + cover_sum)
    last = last.reshape(1, 4096)
    new_enthalpy[...] = offset[...] + factor[...] * last


def local(
    ocean_temp,
    ocean_salt,
    wet_mask,
    vertical_mix,
    friction,
    pressure,
    pair_column,
    pair_weight,
    block_owner,
    block_target,
    enthalpy,
    surface_enthalpy,
    transition_layer,
    column_area,
):
    shape = jax.ShapeDtypeStruct
    ocean = (ocean_temp, ocean_salt, wet_mask, vertical_mix, friction, pressure)
    ocean_specs = [whole(a.shape) for a in ocean]
    count_x = lax.axis_size("gx")
    count_y = lax.axis_size("gy")
    ahead = lambda n: [(i, i + 1) for i in range(n - 1)]
    back = lambda n: [(i + 1, i) for i in range(n - 1)]
    rows_shape = shape((halo_rows, 128), f32)
    up, down = call(
        row_pack_body, (rows_shape, rows_shape), ocean, ocean_specs, cost=(10**5, 10**6)
    )
    bottom = lax.ppermute(up, "gy", back(count_y))
    top = lax.ppermute(down, "gy", ahead(count_y))
    slots_shape = count_x * count_y * slots
    slot_ins = (block_owner, block_target.reshape(1, -1), pair_column, pair_weight)
    slot_row, slot_lane, slot_weight, slot_target = call(
        slot_body,
        (
            shape((slots_shape, 128), jnp.int32),
            shape((slots_shape, 128), jnp.int32),
            shape((slots_shape, 128), f32),
            shape((count_x * count_y, 128), f32),
        ),
        slot_ins,
        [whole(a.shape) for a in slot_ins],
        cost=(2 * 10**9, 3 * 10**6),
    )
    cols_shape = shape((64, 128), f32)
    left, right = call(
        col_pack_body,
        (cols_shape, cols_shape),
        ocean + (top, bottom),
        ocean_specs + [whole((halo_rows, 128))] * 2,
        [pltpu.VMEM((3 * levels + 3, 16, 128), f32)],
        cost=(10**5, 10**6),
    )
    from_right = lax.ppermute(left, "gx", back(count_x))
    from_left = lax.ppermute(right, "gx", ahead(count_x))
    tile = (8, 128)
    few = (4, 8, 128)
    send = call(
        surface_body,
        shape((count_x * count_y * chunk, 128), f32),
        ocean
        + (top,) * 4
        + (bottom,) * 4
        + (from_right, from_left, slot_row, slot_lane, slot_weight, slot_target),
        [part(few, 0, 0, 0)] * 3
        + [part(tile, 0, 0)] * 3
        + [part(tile, b, 0) for b in (0, 16, 32, 48)] * 2
        + [whole((64, 128))] * 2
        + [whole((slots_shape, 128))] * 3
        + [whole((count_x * count_y, 128))],
        [pltpu.VMEM((12, 16, 256), f32)],
        cost=(10**6, 3 * 10**6),
    )
    send, bottom, surface_enthalpy = lax.optimization_barrier((send, bottom, surface_enthalpy))
    got = lax.all_to_all(
        send.reshape(count_x * count_y, chunk, 1, 128),
        ("gx", "gy"),
        split_axis=0,
        concat_axis=0,
        tiled=True,
    ).reshape(count_x * count_y * chunk, 128)
    new_temp, new_salt = call(
        ocean_body,
        (shape(ocean_temp.shape, f32), shape(ocean_salt.shape, f32)),
        ocean + (top, bottom, from_right, from_left),
        ocean_specs + [whole((halo_rows, 128))] * 2 + [whole((64, 128))] * 2,
        [pltpu.VMEM((6, 16, 256), f32), pltpu.VMEM((2, levels, 8, 128), f32)],
        cost=(10**8, 2 * 10**6),
    )
    ice_shape = shape((32, 128), f32)
    column_ins = (enthalpy, surface_enthalpy.reshape(32, 128), transition_layer.reshape(32, 128))
    offset, factor, pivot_end, side_end = call(
        column_body,
        (shape(enthalpy.shape, f32), shape(enthalpy.shape, f32), ice_shape, ice_shape),
        column_ins,
        [whole(a.shape) for a in column_ins],
        cost=(10**8, 2 * 10**6),
    )
    last_ins = (got, column_area.reshape(32, 128), offset, factor, pivot_end, side_end)
    new_enthalpy, melt = call(
        collect_body,
        (shape(enthalpy.shape, f32), ice_shape),
        last_ins,
        [whole(a.shape) for a in last_ins],
        cost=(10**9, 4 * 10**6),
    )
    return new_temp, new_salt, new_enthalpy, melt.reshape(-1)


def solution(mesh):
    return jax.shard_map(
        local,
        mesh=mesh,
        in_specs=(
            P(None, "gy", "gx"),
            P(None, "gy", "gx"),
            P(None, "gy", "gx"),
            P("gy", "gx"),
            P("gy", "gx"),
            P("gy", "gx"),
            P(("gx", "gy"), None),
            P(("gx", "gy"), None),
            P(("gx", "gy"), None),
            P(("gx", "gy")),
            P(None, ("gx", "gy")),
            P(("gx", "gy")),
            P(("gx", "gy")),
            P(("gx", "gy")),
        ),
        out_specs=(
            P(None, "gy", "gx"),
            P(None, "gy", "gx"),
            P(None, ("gx", "gy")),
            P(("gx", "gy")),
        ),
        check_vma=False,
    )
```

```python
import jax
import jax.numpy as jnp
from jax import lax
from jax.experimental import pallas as pl
from jax.experimental.pallas import tpu as pltpu
from jax.sharding import PartitionSpec as P

mixing_rate = 0.2
liquidus_slope = -0.0573
liquidus_base = 0.0832
liquidus_depth = -0.000753
latent_ratio = 4.0
salt_ratio = 35.0
relax_rate = 0.1
cold_rate = 2.0
temperate_rate = 0.2

f32 = jnp.float32
bf16 = jnp.bfloat16
levels = 64
slots = 8
chunk = 3 * slots + 1
halo_rows = 392
few = 3


def lanes_of(shape):
    return lax.broadcasted_iota(jnp.int32, shape, len(shape) - 1)


def call(body, outs, ins, scratch=(), cost=(0, 0)):
    arrays, specs = [], []
    for item in ins:
        if isinstance(item, Near):
            arrays.append(pltpu.with_memory_space_constraint(item.array, pltpu.VMEM))
            specs.append(pl.BlockSpec(memory_space=pltpu.VMEM))
        else:
            array, block, index = item if isinstance(item, tuple) else (item, item.shape, None)
            arrays.append(pltpu.with_memory_space_constraint(array, pltpu.HBM))
            specs.append(part(block, index or (0,) * len(block)))
    out_specs = jax.tree.map(
        lambda o: part(o.shape, (0,) * len(o.shape))
        if isinstance(o, jax.ShapeDtypeStruct)
        else pl.BlockSpec(memory_space=pltpu.VMEM),
        outs,
    )
    return pl.pallas_call(
        body,
        out_shape=outs,
        grid=(1,),
        in_specs=specs,
        out_specs=out_specs,
        scratch_shapes=scratch,
        compiler_params=pltpu.CompilerParams(vmem_limit_bytes=16 << 20),
        cost_estimate=pl.CostEstimate(flops=cost[0], bytes_accessed=cost[1], transcendentals=0),
    )(*arrays)


class Near:
    def __init__(self, array):
        self.array = array


def part(shape, index):
    return pl.BlockSpec(tuple(shape), lambda i: tuple(index))


def all_planes(temp, salt, wet, mix, friction, pressure):
    for source in (temp, salt, wet):
        for k in range(levels):
            yield source[k].astype(f32)
    for source in (mix, friction, pressure):
        yield source[...]


def row_pack(planes, up, down):
    at = 0
    for value in planes:
        up[at : at + 2, :] = value[0:2, :]
        down[at : at + 2, :] = value[6:8, :]
        at += 2
    if at < up.shape[0]:
        up[at:, :] = jnp.zeros((up.shape[0] - at, 128), f32)
        down[at:, :] = jnp.zeros((up.shape[0] - at, 128), f32)


def all_rows_body(temp, salt, wet, mix, friction, pressure, up, down):
    row_pack(all_planes(temp, salt, wet, mix, friction, pressure), up, down)


def col_pack(planes, groups, top, bottom, left, right, tall):
    zeros = jnp.zeros((8, 128), f32)
    half = lanes_of((16, 128)) // 2
    for at, value in enumerate(planes):
        tall[at, 0:8, :] = value
        tall[at, 8:16, :] = zeros
        tall[at, 8:10, :] = bottom[2 * at : 2 * at + 2, :]
        tall[at, 14:16, :] = top[2 * at : 2 * at + 2, :]
    start = 0
    for group, count in enumerate(groups):
        go_left = jnp.zeros((16, 128), f32)
        go_right = jnp.zeros((16, 128), f32)
        for k in range(count):
            value = tall[start + k]
            here = half == k
            go_left = jnp.where(here, pltpu.roll(value, 2 * k, 1), go_left)
            go_right = jnp.where(here, pltpu.roll(value, (2 * k + 2) % 128, 1), go_right)
        left[16 * group : 16 * group + 16, :] = go_left
        right[16 * group : 16 * group + 16, :] = go_right
        start += count


def all_cols_body(temp, salt, wet, mix, friction, pressure, top, bottom, left, right, tall):
    planes = all_planes(temp, salt, wet, mix, friction, pressure)
    col_pack(planes, (levels, levels, levels, 3), top, bottom, left, right, tall)


def extended(tall, from_right, from_left, k, dry=False):
    lane = lanes_of((16, 128))
    side = jnp.where(
        lane < 64,
        pltpu.roll(from_right, (128 - 2 * k) % 128, 1),
        pltpu.roll(from_left, 126 - 2 * k, 1),
    )
    if dry:
        side = jnp.where((lane < 2) | (lane >= 126), side, 0.0)
    return jnp.concatenate([tall, side], axis=1)


def beside(value):
    rows, cols = value.shape
    return (
        pltpu.roll(value, 1, 0),
        pltpu.roll(value, rows - 1, 0),
        pltpu.roll(value, 1, 1),
        pltpu.roll(value, cols - 1, 1),
    )


def spread(value, links):
    change = jnp.zeros_like(value)
    for link, near in zip(links, beside(value)):
        change = change + link * (near - value)
    return value + mixing_rate * change


def links_of(wet):
    return tuple(wet * near for near in beside(wet))


def shelf_melt(surface_temp, surface_salt, friction, pressure, wet_top):
    heat_gain = jnp.where(wet_top > 0, friction, 1.0)
    salt_safe = jnp.where(wet_top > 0, surface_salt, 34.0)
    salt_gain = heat_gain / salt_ratio
    curvature = heat_gain * liquidus_slope
    linear = (
        heat_gain * (surface_temp - liquidus_base - liquidus_depth * pressure)
        + latent_ratio * salt_gain
    )
    constant = latent_ratio * salt_gain * salt_safe
    boundary_salt = (
        2.0 * constant / (linear + jnp.sqrt(linear * linear - 4.0 * curvature * constant))
    )
    boundary_temp = liquidus_slope * boundary_salt + liquidus_base + liquidus_depth * pressure
    heat_flux = heat_gain * (surface_temp - boundary_temp) * wet_top
    salt_flux = salt_gain * (salt_safe - boundary_salt) * wet_top
    return heat_flux, salt_flux, boundary_temp * wet_top


def centre_of(value):
    return value[0:8, 0:128]


def surface_body(
    tall, from_right, from_left, slot_row, slot_lane, slot_weight, slot_target, send
):
    def plane(group, k):
        rows = slice(16 * group, 16 * group + 16)
        value = tall[group * levels + k]
        return extended(value, from_right[rows, :], from_left[rows, :], k, group == 2)

    planes = [plane(group, k) for group in range(3) for k in range(few)]
    planes += [plane(3, place) for place in range(3)]
    wets = planes[2 * few : 3 * few]
    mixing, rub, press = planes[9:12]
    first = mixing * (wets[0] * wets[1])
    second = mixing * (wets[1] * wets[2])
    links = [links_of(value) for value in wets]
    stepped = []
    for field in range(2):
        near = [spread(planes[few * field + k], links[k]) for k in range(few)]
        flux = first * (near[1] - near[0])
        under = second * (near[2] - near[1])
        stepped.append((near[0] + flux, near[1] + under - flux))
    heat, brine, base_one = shelf_melt(stepped[0][0], stepped[1][0], rub, press, wets[0])
    tops = (stepped[0][0] - relax_rate * heat, stepped[1][0] - relax_rate * brine)
    later = []
    for field in range(2):
        near0 = spread(tops[field], links[0])
        near1 = spread(stepped[field][1], links[1])
        later.append(centre_of(near0 + first * (near1 - near0)))
    heat_two, unused, base_two = shelf_melt(
        later[0], later[1], centre_of(rub), centre_of(press), centre_of(wets[0])
    )
    melt = 0.5 * (centre_of(heat) / latent_ratio + heat_two / latent_ratio)
    base = 0.5 * (centre_of(base_one) + base_two)

    melts = [jnp.broadcast_to(melt[r : r + 1, :], (8, 128)) for r in range(8)]
    bases = [jnp.broadcast_to(base[r : r + 1, :], (8, 128)) for r in range(8)]

    def owners(i, carry):
        out = send.at[pl.ds(pl.multiple_of(8 * chunk * i, 8), 8 * chunk)]
        for j in range(8):
            at = pl.ds(pl.multiple_of(64 * i + 8 * j, 8), 8)
            lane = slot_lane[at, :]
            row = slot_row[at, :]
            weight = slot_weight[at, :]
            melt_here = jnp.take_along_axis(melts[0], lane, axis=1)
            base_here = jnp.take_along_axis(bases[0], lane, axis=1)
            for r in range(1, 8):
                hit = row == r
                melt_here = jnp.where(
                    hit, jnp.take_along_axis(melts[r], lane, axis=1), melt_here
                )
                base_here = jnp.where(
                    hit, jnp.take_along_axis(bases[r], lane, axis=1), base_here
                )
            out[chunk * j : chunk * j + 8, :] = weight * melt_here
            out[chunk * j + 8 : chunk * j + 16, :] = weight * base_here
            out[chunk * j + 16 : chunk * j + 24, :] = weight
        targets = slot_target[pl.ds(pl.multiple_of(8 * i, 8), 8), :]
        for j in range(8):
            out[chunk * j + 24 : chunk * j + 25, :] = targets[j : j + 1, :]
        return carry

    lax.fori_loop(0, 16, owners, 0)


def slot_body(owner, target, column, weight, slot_row, slot_lane, slot_weight, slot_target):
    count = owner.shape[1]
    row = lax.broadcasted_iota(jnp.int32, (count, count), 0)
    col = lax.broadcasted_iota(jnp.int32, (count, count), 1)
    same = row == col
    owner_lane = owner[...]
    alike = jnp.sum(jnp.where(same, owner_lane, 0), axis=1, keepdims=True) == owner_lane
    rank_lane = jnp.sum(jnp.where(alike & (row < col), 1, 0), axis=0, keepdims=True)
    rank_row = jnp.sum(jnp.where(alike & (col < row), 1, 0), axis=1, keepdims=True)
    target_row = jnp.sum(jnp.where(same, target[...], 0), axis=1, keepdims=True)
    slot = owner_lane * slots + rank_lane
    total = slot_row.shape[0]
    pick = jnp.where(lax.broadcasted_iota(jnp.int32, (total, count), 0) == slot, 1.0, 0.0)
    value = weight[...]
    high = value.astype(bf16)
    rest = value - high.astype(f32)
    middle = rest.astype(bf16)
    low = (rest - middle.astype(f32)).astype(bf16)
    places = column[...]
    table = jnp.concatenate(
        [
            high,
            middle,
            low,
            (places // 128).astype(f32).astype(bf16),
            (places % 128).astype(f32).astype(bf16),
        ],
        axis=1,
    )
    sorted_ = jnp.dot(pick.astype(bf16), table, preferred_element_type=f32)
    slot_weight[...] = sorted_[:, 0:128] + sorted_[:, 128:256] + sorted_[:, 256:384]
    slot_row[...] = sorted_[:, 384:512].astype(jnp.int32)
    slot_lane[...] = sorted_[:, 512:640].astype(jnp.int32)
    lane = lax.broadcasted_iota(jnp.int32, (count, 128), 1)
    spot = jnp.where(rank_row == lane % slots, target_row, 0).astype(f32).astype(bf16)
    holds = jnp.where(lax.broadcasted_iota(jnp.int32, (128, count), 0) == owner_lane, 1.0, 0.0)
    slot_target[...] = jnp.dot(holds.astype(bf16), spot, preferred_element_type=f32)


def ocean_body(
    tall, from_right, from_left, new_temp, new_salt, near, wets, middle_links, later
):
    for end in (0, levels + 1):
        wets[end] = jnp.zeros((16, 256), f32)
        for field in range(2):
            near[field, end] = jnp.zeros((16, 256), f32)
            later[field, end] = jnp.zeros((8, 128), f32)
    mixing, rub, press = (
        extended(tall[3 * levels + p], from_right[48:64, :], from_left[48:64, :], p)
        for p in range(3)
    )

    def group_of(ref, group):
        return ref[16 * group : 16 * group + 16, :]

    def extend(group, k):
        return extended(
            tall[group * levels + k],
            group_of(from_right, group),
            group_of(from_left, group),
            k,
            group == 2,
        )

    unroll = 4

    def spread_level(k):
        water = extend(2, k)
        links = links_of(water)
        wets[k + 1] = water
        for place, link in enumerate(links):
            middle_links[k, place] = centre_of(link)
        for field in range(2):
            near[field, k + 1] = spread(extend(field, k), links)

    def mix_level(k, top):
        water = wets[k + 1]
        under = mixing * (water * wets[k + 2])
        over = mixing * (wets[k] * water)
        once = []
        for field in range(2):
            value = near[field, k + 1]
            value_under = under * (near[field, k + 2] - value)
            value_over = over * (value - near[field, k])
            once.append(value + value_under - value_over)
        if top:
            heat, brine, unused = shelf_melt(once[0], once[1], rub, press, water)
            once = [once[0] - relax_rate * heat, once[1] - relax_rate * brine]
        for field in range(2):
            change = jnp.zeros((8, 128), f32)
            middle = centre_of(once[field])
            for place, side in enumerate(beside(once[field])):
                change = change + middle_links[k, place] * (centre_of(side) - middle)
            later[field, k + 1] = middle + mixing_rate * change

    def finish_level(k, top):
        water = centre_of(wets[k + 1])
        mixing_c = centre_of(mixing)
        under = mixing_c * (water * centre_of(wets[k + 2]))
        over = mixing_c * (centre_of(wets[k]) * water)
        done = []
        for field in range(2):
            value = later[field, k + 1]
            value_under = under * (later[field, k + 2] - value)
            value_over = over * (value - later[field, k])
            done.append(value + value_under - value_over)
        if top:
            heat, brine, unused = shelf_melt(
                done[0], done[1], centre_of(rub), centre_of(press), water
            )
            done = [done[0] - relax_rate * heat, done[1] - relax_rate * brine]
        new_temp[k] = done[0]
        new_salt[k] = done[1]

    def every(step):
        def several(i, carry):
            for j in range(unroll):
                step(unroll * i + j)
            return carry

        lax.fori_loop(0, levels // unroll, several, 0)

    every(spread_level)
    every(lambda k: mix_level(k, False))
    mix_level(0, True)
    every(lambda k: finish_level(k, False))
    finish_level(0, True)


def column_body(enthalpy, surface, transition, offset, factor, pivot_end, side_end):
    count = enthalpy.shape[0]
    side = enthalpy[...].reshape(count, 32, 128)
    change_at = transition[...]
    rates = [jnp.where(k < change_at, cold_rate, temperate_rate) for k in range(count)]
    inner = [0.5 * (rates[k] + rates[k + 1]) for k in range(count - 1)]
    ratios = []
    values = []
    for k in range(count - 1):
        if k == 0:
            pivot = 1.0 + rates[0] + inner[0]
            right = side[0] + rates[0] * surface[...]
        else:
            pivot = 1.0 + inner[k - 1] + inner[k] + inner[k - 1] * ratios[-1]
            right = side[k] + inner[k - 1] * values[-1]
        scale = 1.0 / pivot
        ratios.append(-inner[k] * scale)
        values.append(right * scale)
    pivot_end[...] = 1.0 + inner[-1] + inner[-1] * ratios[-1]
    side_end[...] = side[count - 1] + inner[-1] * values[-1]
    offsets = [jnp.zeros((32, 128), f32)]
    factors = [jnp.ones((32, 128), f32)]
    for k in range(count - 2, -1, -1):
        offsets.append(values[k] - ratios[k] * offsets[-1])
        factors.append(-ratios[k] * factors[-1])
    offset[...] = jnp.stack(offsets[::-1]).reshape(count, 4096)
    factor[...] = jnp.stack(factors[::-1]).reshape(count, 4096)


def collect_body(got, area, offset, factor, pivot_end, side_end, new_enthalpy, melt):
    sums = jnp.zeros((32, 384), f32)
    lane = lax.broadcasted_iota(jnp.int32, (1, 128), 1) // slots
    wanted = lax.broadcasted_iota(jnp.int32, (32, 128), 0).astype(f32)
    for group in range(8):
        parts = ([], [], [])
        target = jnp.zeros((1, 128), f32)
        for s in range(16):
            at = chunk * (16 * group + s)
            for place in range(3):
                parts[place].append(got[at + 8 * place : at + 8 * place + 8, :])
            target = jnp.where(lane == s, got[at + 24 : at + 25, :], target)
        hot = jnp.where(wanted == target, 1.0, 0.0).astype(bf16)
        value = jnp.concatenate([jnp.concatenate(p, axis=0) for p in parts], axis=1)
        high = value.astype(bf16)
        rest = value - high.astype(f32)
        middle = rest.astype(bf16)
        low = (rest - middle.astype(f32)).astype(bf16)
        for piece in (high, middle, low):
            sums = sums + jnp.dot(hot, piece, preferred_element_type=f32)
    size = area[...]
    melt[...] = sums[:, 0:128] / size
    base_sum = sums[:, 128:256] / size
    cover_sum = sums[:, 256:384] / size
    last = (side_end[...] + base_sum) / (pivot_end[...] + cover_sum)
    last = last.reshape(1, 4096)
    new_enthalpy[...] = offset[...] + factor[...] * last


def local(
    ocean_temp,
    ocean_salt,
    wet_mask,
    vertical_mix,
    friction,
    pressure,
    pair_column,
    pair_weight,
    block_owner,
    block_target,
    enthalpy,
    surface_enthalpy,
    transition_layer,
    column_area,
):
    shape = jax.ShapeDtypeStruct
    ocean = (ocean_temp, ocean_salt, wet_mask, vertical_mix, friction, pressure)
    count_x = lax.axis_size("gx")
    count_y = lax.axis_size("gy")
    devices = count_x * count_y

    def chip(*dims, dtype=f32):
        return pltpu.VMEM(dims, dtype)

    def exchange(low, high, axis, count):
        ahead = [(i, i + 1) for i in range(count - 1)]
        back = [(i + 1, i) for i in range(count - 1)]
        return lax.ppermute(low, axis, back), lax.ppermute(high, axis, ahead)

    up, down = call(
        all_rows_body, (chip(halo_rows, 128), chip(halo_rows, 128)), ocean, cost=(10**5, 10**6)
    )
    bottom, top = exchange(up, down, "gy", count_y)
    slot_row, slot_lane, slot_weight, slot_target = call(
        slot_body,
        (
            chip(devices * slots, 128, dtype=jnp.int32),
            chip(devices * slots, 128, dtype=jnp.int32),
            chip(devices * slots, 128),
            chip(devices, 128),
        ),
        (block_owner.reshape(1, -1), block_target.reshape(1, -1), pair_column, pair_weight),
        cost=(2 * 10**9, 3 * 10**6),
    )
    top, slot_target = lax.optimization_barrier((top, slot_target))
    left, right, tall = call(
        all_cols_body,
        (chip(64, 128), chip(64, 128), chip(3 * levels + 3, 16, 128)),
        ocean + (Near(top), Near(bottom)),
        cost=(10**5, 10**6),
    )
    from_right, from_left = exchange(left, right, "gx", count_x)
    send = call(
        surface_body,
        chip(devices * chunk, 128),
        tuple(
            Near(a)
            for a in (tall, from_right, from_left, slot_row, slot_lane, slot_weight, slot_target)
        ),
        cost=(10**6, 3 * 10**6),
    )
    send, from_left, surface_enthalpy = lax.optimization_barrier(
        (send, from_left, surface_enthalpy)
    )
    got = lax.all_to_all(
        send.reshape(devices, chunk, 1, 128),
        ("gx", "gy"),
        split_axis=0,
        concat_axis=0,
        tiled=True,
    ).reshape(devices * chunk, 128)
    new_temp, new_salt = call(
        ocean_body,
        (shape(ocean_temp.shape, f32), shape(ocean_salt.shape, f32)),
        (Near(tall), Near(from_right), Near(from_left)),
        [
            pltpu.VMEM((2, levels + 2, 16, 256), f32),
            pltpu.VMEM((levels + 2, 16, 256), f32),
            pltpu.VMEM((levels, 4, 8, 128), f32),
            pltpu.VMEM((2, levels + 2, 8, 128), f32),
        ],
        cost=(10**8, 2 * 10**6),
    )
    new_temp, surface_enthalpy = lax.optimization_barrier((new_temp, surface_enthalpy))
    offset, factor, pivot_end, side_end = call(
        column_body,
        (chip(*enthalpy.shape), chip(*enthalpy.shape), chip(32, 128), chip(32, 128)),
        (enthalpy, surface_enthalpy.reshape(32, 128), transition_layer.reshape(32, 128)),
        cost=(10**8, 2 * 10**6),
    )
    new_enthalpy, melt = call(
        collect_body,
        (shape(enthalpy.shape, f32), shape((32, 128), f32)),
        (
            Near(got),
            column_area.reshape(32, 128),
            Near(offset),
            Near(factor),
            Near(pivot_end),
            Near(side_end),
        ),
        cost=(10**9, 4 * 10**6),
    )
    return new_temp, new_salt, new_enthalpy, melt.reshape(-1)


def solution(mesh):
    return jax.shard_map(
        local,
        mesh=mesh,
        in_specs=(
            P(None, "gy", "gx"),
            P(None, "gy", "gx"),
            P(None, "gy", "gx"),
            P("gy", "gx"),
            P("gy", "gx"),
            P("gy", "gx"),
            P(("gx", "gy"), None),
            P(("gx", "gy"), None),
            P(("gx", "gy"), None),
            P(("gx", "gy")),
            P(None, ("gx", "gy")),
            P(("gx", "gy")),
            P(("gx", "gy")),
            P(("gx", "gy")),
        ),
        out_specs=(
            P(None, "gy", "gx"),
            P(None, "gy", "gx"),
            P(None, ("gx", "gy")),
            P(("gx", "gy")),
        ),
        check_vma=False,
    )
```

```python
import jax
import jax.numpy as jnp
from jax import lax
from jax.experimental import pallas as pl
from jax.experimental.pallas import tpu as pltpu
from jax.sharding import PartitionSpec as P

mixing_rate = 0.2
liquidus_slope = -0.0573
liquidus_base = 0.0832
liquidus_depth = -0.000753
latent_ratio = 4.0
salt_ratio = 35.0
relax_rate = 0.1
cold_rate = 2.0
temperate_rate = 0.2

f32 = jnp.float32
bf16 = jnp.bfloat16
levels = 64
slots = 8
chunk = 3 * slots + 1
halo_rows = 392
few = 3
batch = 16


def lanes_of(shape):
    return lax.broadcasted_iota(jnp.int32, shape, len(shape) - 1)


def call(body, outs, ins, scratch=(), cost=(0, 0), own_copies=False):
    arrays, specs = [], []
    for item in ins:
        if isinstance(item, Near):
            arrays.append(pltpu.with_memory_space_constraint(item.array, pltpu.VMEM))
            specs.append(pl.BlockSpec(memory_space=pltpu.VMEM))
        else:
            array, block, index = item if isinstance(item, tuple) else (item, item.shape, None)
            arrays.append(pltpu.with_memory_space_constraint(array, pltpu.HBM))
            specs.append(part(block, index or (0,) * len(block)))
    if own_copies:
        out_specs = pl.BlockSpec(memory_space=pltpu.HBM)
    else:
        out_specs = jax.tree.map(
            lambda o: part(o.shape, (0,) * len(o.shape))
            if isinstance(o, jax.ShapeDtypeStruct)
            else pl.BlockSpec(memory_space=pltpu.VMEM),
            outs,
        )
    return pl.pallas_call(
        body,
        out_shape=outs,
        grid=(1,),
        in_specs=specs,
        out_specs=out_specs,
        scratch_shapes=scratch,
        compiler_params=pltpu.CompilerParams(vmem_limit_bytes=16 << 20),
        cost_estimate=pl.CostEstimate(flops=cost[0], bytes_accessed=cost[1], transcendentals=0),
    )(*arrays)


class Near:
    def __init__(self, array):
        self.array = array


def part(shape, index):
    return pl.BlockSpec(tuple(shape), lambda i: tuple(index))


def all_planes(temp, salt, wet, mix, friction, pressure):
    for source in (temp, salt, wet):
        for k in range(levels):
            yield source[k].astype(f32)
    for source in (mix, friction, pressure):
        yield source[...]


def even_on(axis):
    return lax.axis_index(axis) % 2 == 0


def row_pack(planes, first, second):
    even = even_on("gy")
    at = 0
    for value in planes:
        high, low = value[6:8, :], value[0:2, :]
        first[at : at + 2, :] = jnp.where(even, high, low)
        second[at : at + 2, :] = jnp.where(even, low, high)
        at += 2
    first[at:, :] = jnp.zeros((first.shape[0] - at, 128), f32)
    second[at:, :] = jnp.zeros((first.shape[0] - at, 128), f32)


def all_rows_body(temp, salt, wet, mix, friction, pressure, first, second):
    row_pack(all_planes(temp, salt, wet, mix, friction, pressure), first, second)


def col_pack(planes, groups, rows_first, rows_second, first, second, tall):
    zeros = jnp.zeros((8, 128), f32)
    half = lanes_of((16, 128)) // 2
    at_first = jnp.where(even_on("gy"), 8, 14)
    at_second = 22 - at_first
    for at, value in enumerate(planes):
        tall[at, 0:8, :] = value
        tall[at, 8:16, :] = zeros
        tall[at, pl.ds(at_first, 2), :] = rows_first[2 * at : 2 * at + 2, :]
        tall[at, pl.ds(at_second, 2), :] = rows_second[2 * at : 2 * at + 2, :]
    even = even_on("gx")
    start = 0
    for group, count in enumerate(groups):
        low = jnp.zeros((16, 128), f32)
        high = jnp.zeros((16, 128), f32)
        for k in range(count):
            value = tall[start + k]
            here = half == k
            low = jnp.where(here, pltpu.roll(value, 2 * k, 1), low)
            high = jnp.where(here, pltpu.roll(value, (2 * k + 2) % 128, 1), high)
        first[16 * group : 16 * group + 16, :] = jnp.where(even, high, low)
        second[16 * group : 16 * group + 16, :] = jnp.where(even, low, high)
        start += count


def sides_received(first, second):
    even = even_on("gx")
    return jnp.where(even, first, second), jnp.where(even, second, first)


def all_cols_body(temp, salt, wet, mix, friction, pressure, rows_first, rows_second, first, second, tall):
    planes = all_planes(temp, salt, wet, mix, friction, pressure)
    groups = (levels, levels, levels, 3)
    col_pack(planes, groups, rows_first, rows_second, first, second, tall)


def extended(tall, from_right, from_left, k, dry=False):
    lane = lanes_of((16, 128))
    side = jnp.where(
        lane < 64,
        pltpu.roll(from_right, (128 - 2 * k) % 128, 1),
        pltpu.roll(from_left, 126 - 2 * k, 1),
    )
    if dry:
        side = jnp.where((lane < 2) | (lane >= 126), side, 0.0)
    return jnp.concatenate([tall, side], axis=1)


def beside(value):
    rows, cols = value.shape
    return (
        pltpu.roll(value, 1, 0),
        pltpu.roll(value, rows - 1, 0),
        pltpu.roll(value, 1, 1),
        pltpu.roll(value, cols - 1, 1),
    )


def spread(value, links):
    change = jnp.zeros_like(value)
    for link, near in zip(links, beside(value)):
        change = change + link * (near - value)
    return value + mixing_rate * change


def links_of(wet):
    return tuple(wet * near for near in beside(wet))


def shelf_melt(surface_temp, surface_salt, friction, pressure, wet_top):
    heat_gain = jnp.where(wet_top > 0, friction, 1.0)
    salt_safe = jnp.where(wet_top > 0, surface_salt, 34.0)
    salt_gain = heat_gain / salt_ratio
    curvature = heat_gain * liquidus_slope
    linear = (
        heat_gain * (surface_temp - liquidus_base - liquidus_depth * pressure)
        + latent_ratio * salt_gain
    )
    constant = latent_ratio * salt_gain * salt_safe
    boundary_salt = (
        2.0 * constant / (linear + jnp.sqrt(linear * linear - 4.0 * curvature * constant))
    )
    boundary_temp = liquidus_slope * boundary_salt + liquidus_base + liquidus_depth * pressure
    heat_flux = heat_gain * (surface_temp - boundary_temp) * wet_top
    salt_flux = salt_gain * (salt_safe - boundary_salt) * wet_top
    return heat_flux, salt_flux, boundary_temp * wet_top


def centre_of(value):
    return value[0:8, 0:128]


def surface_body(
    tall, cols_first, cols_second, slot_row, slot_lane, slot_weight, slot_target, send, held, sems
):
    from_right, from_left = sides_received(cols_first[...], cols_second[...])

    def plane(group, k):
        rows = slice(16 * group, 16 * group + 16)
        value = tall[group * levels + k]
        return extended(value, from_right[rows], from_left[rows], k, group == 2)

    planes = [plane(group, k) for group in range(3) for k in range(few)]
    planes += [plane(3, place) for place in range(3)]
    wets = planes[2 * few : 3 * few]
    mixing, rub, press = planes[9:12]
    first = mixing * (wets[0] * wets[1])
    second = mixing * (wets[1] * wets[2])
    links = [links_of(value) for value in wets]
    stepped = []
    for field in range(2):
        near = [spread(planes[few * field + k], links[k]) for k in range(few)]
        flux = first * (near[1] - near[0])
        under = second * (near[2] - near[1])
        stepped.append((near[0] + flux, near[1] + under - flux))
    heat, brine, base_one = shelf_melt(stepped[0][0], stepped[1][0], rub, press, wets[0])
    tops = (stepped[0][0] - relax_rate * heat, stepped[1][0] - relax_rate * brine)
    later = []
    for field in range(2):
        near0 = spread(tops[field], links[0])
        near1 = spread(stepped[field][1], links[1])
        later.append(centre_of(near0 + first * (near1 - near0)))
    heat_two, unused, base_two = shelf_melt(
        later[0], later[1], centre_of(rub), centre_of(press), centre_of(wets[0])
    )
    melt = 0.5 * (centre_of(heat) / latent_ratio + heat_two / latent_ratio)
    base = 0.5 * (centre_of(base_one) + base_two)

    melts = [jnp.broadcast_to(melt[r : r + 1, :], (8, 128)) for r in range(8)]
    bases = [jnp.broadcast_to(base[r : r + 1, :], (8, 128)) for r in range(8)]

    def leave(i):
        rows = pl.ds(pl.multiple_of(chunk * batch * i, 8), chunk * batch)
        return pltpu.make_async_copy(held.at[rows], send.at[rows], sems.at[i])

    def owners(i, carry):
        out = held.at[pl.ds(pl.multiple_of(chunk * batch * i, 8), chunk * batch)]
        targets = slot_target[pl.ds(pl.multiple_of(batch * i, 8), batch), :]
        for j in range(batch):
            at = pl.ds(pl.multiple_of(8 * batch * i + 8 * j, 8), 8)
            lane = slot_lane[at, :]
            row = slot_row[at, :]
            weight = slot_weight[at, :]
            melt_here = jnp.take_along_axis(melts[0], lane, axis=1)
            base_here = jnp.take_along_axis(bases[0], lane, axis=1)
            for r in range(1, 8):
                hit = row == r
                melt_here = jnp.where(
                    hit, jnp.take_along_axis(melts[r], lane, axis=1), melt_here
                )
                base_here = jnp.where(
                    hit, jnp.take_along_axis(bases[r], lane, axis=1), base_here
                )
            out[chunk * j : chunk * j + 8, :] = weight * melt_here
            out[chunk * j + 8 : chunk * j + 16, :] = weight * base_here
            out[chunk * j + 16 : chunk * j + 24, :] = weight
            out[chunk * j + 24 : chunk * j + 25, :] = targets[j : j + 1, :]
        leave(i).start()
        return carry

    count = slot_target.shape[0] // batch
    lax.fori_loop(0, count, owners, 0)
    for i in range(count):
        leave(i).wait()


def slot_body(owner, target, column, weight, slot_row, slot_lane, slot_weight, slot_target):
    count = owner.shape[1]
    row = lax.broadcasted_iota(jnp.int32, (count, count), 0)
    col = lax.broadcasted_iota(jnp.int32, (count, count), 1)
    same = row == col
    owner_lane = owner[...]
    alike = jnp.sum(jnp.where(same, owner_lane, 0), axis=1, keepdims=True) == owner_lane
    rank_lane = jnp.sum(jnp.where(alike & (row < col), 1, 0), axis=0, keepdims=True)
    rank_row = jnp.sum(jnp.where(alike & (col < row), 1, 0), axis=1, keepdims=True)
    target_row = jnp.sum(jnp.where(same, target[...], 0), axis=1, keepdims=True)
    slot = owner_lane * slots + rank_lane
    total = slot_row.shape[0]
    pick = jnp.where(lax.broadcasted_iota(jnp.int32, (total, count), 0) == slot, 1.0, 0.0)
    value = weight[...]
    high = value.astype(bf16)
    rest = value - high.astype(f32)
    middle = rest.astype(bf16)
    low = (rest - middle.astype(f32)).astype(bf16)
    places = column[...]
    table = jnp.concatenate(
        [
            high,
            middle,
            low,
            (places // 128).astype(f32).astype(bf16),
            (places % 128).astype(f32).astype(bf16),
        ],
        axis=1,
    )
    sorted_ = jnp.dot(pick.astype(bf16), table, preferred_element_type=f32)
    slot_weight[...] = sorted_[:, 0:128] + sorted_[:, 128:256] + sorted_[:, 256:384]
    slot_row[...] = sorted_[:, 384:512].astype(jnp.int32)
    slot_lane[...] = sorted_[:, 512:640].astype(jnp.int32)
    lane = lax.broadcasted_iota(jnp.int32, (count, 128), 1)
    spot = jnp.where(rank_row == lane % slots, target_row, 0).astype(f32).astype(bf16)
    holds = jnp.where(lax.broadcasted_iota(jnp.int32, (128, count), 0) == owner_lane, 1.0, 0.0)
    slot_target[...] = jnp.dot(holds.astype(bf16), spot, preferred_element_type=f32)


def ocean_body(
    tall,
    cols_first,
    cols_second,
    new_temp,
    new_salt,
    near,
    wets,
    middle_links,
    later,
    from_right,
    from_left,
):
    from_right[...], from_left[...] = sides_received(cols_first[...], cols_second[...])
    for end in (0, levels + 1):
        wets[end] = jnp.zeros((16, 256), f32)
        for field in range(2):
            near[field, end] = jnp.zeros((16, 256), f32)
            later[field, end] = jnp.zeros((8, 128), f32)
    mixing, rub, press = (
        extended(tall[3 * levels + p], from_right[48:64, :], from_left[48:64, :], p)
        for p in range(3)
    )

    def group_of(ref, group):
        return ref[16 * group : 16 * group + 16, :]

    def extend(group, k):
        return extended(
            tall[group * levels + k],
            group_of(from_right, group),
            group_of(from_left, group),
            k,
            group == 2,
        )

    unroll = 4

    def spread_level(k):
        water = extend(2, k)
        links = links_of(water)
        wets[k + 1] = water
        for place, link in enumerate(links):
            middle_links[k, place] = centre_of(link)
        for field in range(2):
            near[field, k + 1] = spread(extend(field, k), links)

    def mix_level(k, top):
        water = wets[k + 1]
        under = mixing * (water * wets[k + 2])
        over = mixing * (wets[k] * water)
        once = []
        for field in range(2):
            value = near[field, k + 1]
            value_under = under * (near[field, k + 2] - value)
            value_over = over * (value - near[field, k])
            once.append(value + value_under - value_over)
        if top:
            heat, brine, unused = shelf_melt(once[0], once[1], rub, press, water)
            once = [once[0] - relax_rate * heat, once[1] - relax_rate * brine]
        for field in range(2):
            change = jnp.zeros((8, 128), f32)
            middle = centre_of(once[field])
            for place, side in enumerate(beside(once[field])):
                change = change + middle_links[k, place] * (centre_of(side) - middle)
            later[field, k + 1] = middle + mixing_rate * change

    def finish_level(k, top):
        water = centre_of(wets[k + 1])
        mixing_c = centre_of(mixing)
        under = mixing_c * (water * centre_of(wets[k + 2]))
        over = mixing_c * (centre_of(wets[k]) * water)
        done = []
        for field in range(2):
            value = later[field, k + 1]
            value_under = under * (later[field, k + 2] - value)
            value_over = over * (value - later[field, k])
            done.append(value + value_under - value_over)
        if top:
            heat, brine, unused = shelf_melt(
                done[0], done[1], centre_of(rub), centre_of(press), water
            )
            done = [done[0] - relax_rate * heat, done[1] - relax_rate * brine]
        new_temp[k] = done[0]
        new_salt[k] = done[1]

    def every(step):
        def several(i, carry):
            for j in range(unroll):
                step(unroll * i + j)
            return carry

        lax.fori_loop(0, levels // unroll, several, 0)

    every(spread_level)
    every(lambda k: mix_level(k, False))
    mix_level(0, True)
    every(lambda k: finish_level(k, False))
    finish_level(0, True)


def column_body(enthalpy, surface, transition, offset, factor, pivot_end, side_end):
    count = enthalpy.shape[0]
    side = enthalpy[...].reshape(count, 32, 128)
    change_at = transition[...]
    rates = [jnp.where(k < change_at, cold_rate, temperate_rate) for k in range(count)]
    inner = [0.5 * (rates[k] + rates[k + 1]) for k in range(count - 1)]
    ratios = []
    values = []
    for k in range(count - 1):
        if k == 0:
            pivot = 1.0 + rates[0] + inner[0]
            right = side[0] + rates[0] * surface[...]
        else:
            pivot = 1.0 + inner[k - 1] + inner[k] + inner[k - 1] * ratios[-1]
            right = side[k] + inner[k - 1] * values[-1]
        scale = 1.0 / pivot
        ratios.append(-inner[k] * scale)
        values.append(right * scale)
    pivot_end[...] = 1.0 + inner[-1] + inner[-1] * ratios[-1]
    side_end[...] = side[count - 1] + inner[-1] * values[-1]
    offsets = [jnp.zeros((32, 128), f32)]
    factors = [jnp.ones((32, 128), f32)]
    for k in range(count - 2, -1, -1):
        offsets.append(values[k] - ratios[k] * offsets[-1])
        factors.append(-ratios[k] * factors[-1])
    offset[...] = jnp.stack(offsets[::-1]).reshape(count, 4096)
    factor[...] = jnp.stack(factors[::-1]).reshape(count, 4096)


def collect_body(got, area, offset, factor, pivot_end, side_end, new_enthalpy, melt):
    sums = jnp.zeros((32, 384), f32)
    lane = lax.broadcasted_iota(jnp.int32, (1, 128), 1) // slots
    wanted = lax.broadcasted_iota(jnp.int32, (32, 128), 0).astype(f32)
    for group in range(8):
        parts = ([], [], [])
        target = jnp.zeros((1, 128), f32)
        for s in range(16):
            at = chunk * (16 * group + s)
            for place in range(3):
                parts[place].append(got[at + 8 * place : at + 8 * place + 8, :])
            target = jnp.where(lane == s, got[at + 24 : at + 25, :], target)
        hot = jnp.where(wanted == target, 1.0, 0.0).astype(bf16)
        value = jnp.concatenate([jnp.concatenate(p, axis=0) for p in parts], axis=1)
        high = value.astype(bf16)
        rest = value - high.astype(f32)
        middle = rest.astype(bf16)
        low = (rest - middle.astype(f32)).astype(bf16)
        for piece in (high, middle, low):
            sums = sums + jnp.dot(hot, piece, preferred_element_type=f32)
    size = area[...]
    melt[...] = sums[:, 0:128] / size
    base_sum = sums[:, 128:256] / size
    cover_sum = sums[:, 256:384] / size
    last = (side_end[...] + base_sum) / (pivot_end[...] + cover_sum)
    last = last.reshape(1, 4096)
    new_enthalpy[...] = offset[...] + factor[...] * last


def local(
    ocean_temp,
    ocean_salt,
    wet_mask,
    vertical_mix,
    friction,
    pressure,
    pair_column,
    pair_weight,
    block_owner,
    block_target,
    enthalpy,
    surface_enthalpy,
    transition_layer,
    column_area,
):
    shape = jax.ShapeDtypeStruct
    ocean = (ocean_temp, ocean_salt, wet_mask, vertical_mix, friction, pressure)
    count_x = lax.axis_size("gx")
    count_y = lax.axis_size("gy")
    devices = count_x * count_y

    def chip(*dims, dtype=f32):
        return pltpu.VMEM(dims, dtype)

    def exchange(first, second, axis, count):
        pairs = [(i, i ^ 1) for i in range(count)]
        later = [(i + 1, (i ^ 1) + 1) for i in range(count - 2)]
        return lax.ppermute(first, axis, pairs), lax.ppermute(second, axis, later)

    rows_first, rows_second = call(
        all_rows_body, (chip(halo_rows, 128), chip(halo_rows, 128)), ocean, cost=(10**5, 10**6)
    )
    rows_first, rows_second = exchange(rows_first, rows_second, "gy", count_y)
    slot_row, slot_lane, slot_weight, slot_target = call(
        slot_body,
        (
            chip(devices * slots, 128, dtype=jnp.int32),
            chip(devices * slots, 128, dtype=jnp.int32),
            chip(devices * slots, 128),
            chip(devices, 128),
        ),
        (block_owner.reshape(1, -1), block_target.reshape(1, -1), pair_column, pair_weight),
        cost=(2 * 10**9, 3 * 10**6),
    )
    rows_first, slot_target = lax.optimization_barrier((rows_first, slot_target))
    cols_first, cols_second, tall = call(
        all_cols_body,
        (chip(64, 128), chip(64, 128), chip(3 * levels + 3, 16, 128)),
        ocean + (Near(rows_first), Near(rows_second)),
        cost=(10**5, 10**6),
    )
    cols_first, cols_second = exchange(cols_first, cols_second, "gx", count_x)
    send = call(
        surface_body,
        shape((devices * chunk, 128), f32),
        tuple(
            Near(a)
            for a in (
                tall,
                cols_first,
                cols_second,
                slot_row,
                slot_lane,
                slot_weight,
                slot_target,
            )
        ),
        [pltpu.VMEM((devices * chunk, 128), f32), pltpu.SemaphoreType.DMA((devices // batch,))],
        cost=(10**6, 3 * 10**6),
        own_copies=True,
    )
    send, cols_first, surface_enthalpy = lax.optimization_barrier(
        (send, cols_first, surface_enthalpy)
    )
    got = lax.all_to_all(
        send.reshape(devices, chunk, 1, 128),
        ("gx", "gy"),
        split_axis=0,
        concat_axis=0,
        tiled=True,
    ).reshape(devices * chunk, 128)
    new_temp, new_salt = call(
        ocean_body,
        (shape(ocean_temp.shape, f32), shape(ocean_salt.shape, f32)),
        (Near(tall), Near(cols_first), Near(cols_second)),
        [
            pltpu.VMEM((2, levels + 2, 16, 256), f32),
            pltpu.VMEM((levels + 2, 16, 256), f32),
            pltpu.VMEM((levels, 4, 8, 128), f32),
            pltpu.VMEM((2, levels + 2, 8, 128), f32),
            pltpu.VMEM((64, 128), f32),
            pltpu.VMEM((64, 128), f32),
        ],
        cost=(10**8, 2 * 10**6),
    )
    new_temp, surface_enthalpy = lax.optimization_barrier((new_temp, surface_enthalpy))
    offset, factor, pivot_end, side_end = call(
        column_body,
        (chip(*enthalpy.shape), chip(*enthalpy.shape), chip(32, 128), chip(32, 128)),
        (enthalpy, surface_enthalpy.reshape(32, 128), transition_layer.reshape(32, 128)),
        cost=(10**8, 2 * 10**6),
    )
    new_enthalpy, melt = call(
        collect_body,
        (shape(enthalpy.shape, f32), shape((32, 128), f32)),
        (
            Near(got),
            column_area.reshape(32, 128),
            Near(offset),
            Near(factor),
            Near(pivot_end),
            Near(side_end),
        ),
        cost=(10**9, 4 * 10**6),
    )
    return new_temp, new_salt, new_enthalpy, melt.reshape(-1)


def solution(mesh):
    return jax.shard_map(
        local,
        mesh=mesh,
        in_specs=(
            P(None, "gy", "gx"),
            P(None, "gy", "gx"),
            P(None, "gy", "gx"),
            P("gy", "gx"),
            P("gy", "gx"),
            P("gy", "gx"),
            P(("gx", "gy"), None),
            P(("gx", "gy"), None),
            P(("gx", "gy"), None),
            P(("gx", "gy")),
            P(None, ("gx", "gy")),
            P(("gx", "gy")),
            P(("gx", "gy")),
            P(("gx", "gy")),
        ),
        out_specs=(
            P(None, "gy", "gx"),
            P(None, "gy", "gx"),
            P(None, ("gx", "gy")),
            P(("gx", "gy")),
        ),
        check_vma=False,
    )
```

```python
import jax
import jax.numpy as jnp
from jax import lax
from jax.experimental import pallas as pl
from jax.experimental.pallas import tpu as pltpu
from jax.sharding import PartitionSpec as P


mixing_rate = 0.2
liquidus_slope = -0.0573
liquidus_base = 0.0832
liquidus_depth = -0.000753
latent_ratio = 4.0
salt_ratio = 35.0
relax_rate = 0.1
cold_rate = 2.0
temperate_rate = 0.2

f32 = jnp.float32
bf16 = jnp.bfloat16
levels = 64
slots = 8
chunk = 3 * slots + 1
halo_rows = 392
few = 3
batch = 16


def lanes_of(shape):
    return lax.broadcasted_iota(jnp.int32, shape, len(shape) - 1)


def call(body, outs, ins, scratch=(), cost=(0, 0), own_copies=False):
    arrays, specs = [], []
    for item in ins:
        if isinstance(item, Near):
            arrays.append(pltpu.with_memory_space_constraint(item.array, pltpu.VMEM))
            specs.append(pl.BlockSpec(memory_space=pltpu.VMEM))
        else:
            array, block, index = item if isinstance(item, tuple) else (item, item.shape, None)
            arrays.append(pltpu.with_memory_space_constraint(array, pltpu.HBM))
            specs.append(part(block, index or (0,) * len(block)))
    if own_copies:
        out_specs = jax.tree.map(lambda o: pl.BlockSpec(memory_space=pltpu.HBM), outs)
    else:
        out_specs = jax.tree.map(
            lambda o: part(o.shape, (0,) * len(o.shape))
            if isinstance(o, jax.ShapeDtypeStruct)
            else pl.BlockSpec(memory_space=pltpu.VMEM),
            outs,
        )
    return pl.pallas_call(
        body,
        out_shape=outs,
        grid=(1,),
        in_specs=specs,
        out_specs=out_specs,
        scratch_shapes=scratch,
        compiler_params=pltpu.CompilerParams(vmem_limit_bytes=16 << 20),
        cost_estimate=pl.CostEstimate(flops=cost[0], bytes_accessed=cost[1], transcendentals=0),
    )(*arrays)


class Near:
    def __init__(self, array):
        self.array = array


def part(shape, index):
    return pl.BlockSpec(tuple(shape), lambda i: tuple(index))


def even_on(axis):
    return lax.axis_index(axis) % 2 == 0


def all_rows_body(temp, salt, wet, mix, friction, pressure, first, second, centre):
    even = even_on("gy")

    def put(at, high, low):
        first[at : at + 2, :] = jnp.where(even, high, low)
        second[at : at + 2, :] = jnp.where(even, low, high)

    at = 0
    for source in (temp, salt, wet):
        for k in range(levels):
            value = source[k].astype(f32)
            centre[at // 2] = value
            put(at, value[6:8, :], value[0:2, :])
            at += 2
    for source in (mix, friction, pressure):
        centre[at // 2] = source[...]
        put(at, source[6:8, :], source[0:2, :])
        at += 2
    put(at, jnp.zeros((2, 128), f32), jnp.zeros((2, 128), f32))


def tall_plane(tall, at, value, rows_first, rows_second, place):
    at_first = jnp.where(even_on("gy"), 8, 14)
    at_second = 22 - at_first
    tall[at, 0:8, :] = value
    tall[at, 8:16, :] = jnp.zeros((8, 128), f32)
    tall[at, pl.ds(at_first, 2), :] = rows_first[2 * place : 2 * place + 2, :]
    tall[at, pl.ds(at_second, 2), :] = rows_second[2 * place : 2 * place + 2, :]


plane_groups = (levels, levels, levels, 3)


def own_columns(centre, low_side, high_side):
    half = lanes_of((8, 128)) // 2
    start = 0
    for group, count in enumerate(plane_groups):
        low = jnp.zeros((8, 128), f32)
        high = jnp.zeros((8, 128), f32)
        for k in range(count):
            value = centre[start + k]
            here = half == k
            low = jnp.where(here, pltpu.roll(value, 2 * k, 1), low)
            high = jnp.where(here, pltpu.roll(value, (2 * k + 2) % 128, 1), high)
        low_side[8 * group : 8 * group + 8, :] = low
        high_side[8 * group : 8 * group + 8, :] = high
        start += count


def all_cols_body(
    centre, low_side, high_side, rows_first, rows_second, first, second, tall
):
    places = [field * levels + k for field in range(3) for k in range(few)]
    places += [3 * levels + p for p in range(3)]
    for at, place in enumerate(places):
        tall_plane(tall, at, centre[place], rows_first, rows_second, place)

    even_x = even_on("gx")
    even_y = even_on("gy")
    lane = lanes_of((8, 128))
    row = lax.broadcasted_iota(jnp.int32, (8, 128), 0)
    ahead = ((lane - row % 2) & 127) // 2 - row // 2

    def put(at, low, high):
        first[at : at + low.shape[0], :] = jnp.where(even_x, high, low)
        second[at : at + low.shape[0], :] = jnp.where(even_x, low, high)

    def row_columns(rows, start, count):
        low = jnp.zeros((8, 128), f32)
        high = jnp.zeros((8, 128), f32)
        for k in range(0, count, 4):
            value = rows[start + 2 * k : start + 2 * k + 8, :]
            here = ahead == k
            turned = pltpu.roll(value, 2 * k, 1, stride=1, stride_axis=0)
            low = jnp.where(here, turned, low)
            if 2 * k + 2 + 7 < 128:
                turned = pltpu.roll(value, 2 * k + 2, 1, stride=1, stride_axis=0)
            else:
                turned = pltpu.roll(turned, 2, 1)
            high = jnp.where(here, turned, high)
        return tuple(
            (
                jnp.sum(jnp.where(row % 2 == 0, value, 0.0), axis=0, keepdims=True),
                pltpu.roll(
                    jnp.sum(jnp.where(row % 2 == 1, value, 0.0), axis=0, keepdims=True), 127, 1
                ),
            )
            for value in (low, high)
        )

    for group in range(4):
        own = slice(8 * group, 8 * group + 8)
        put(16 * group, low_side[own, :], high_side[own, :])
        put(16 * group + 8, jnp.zeros((8, 128), f32), jnp.zeros((8, 128), f32))
        padded = levels if group < 3 else 4
        one = row_columns(rows_first, 2 * group * levels, padded)
        two = row_columns(rows_second, 2 * group * levels, padded)
        for r in range(2):
            pairs = tuple((a[r], b[r]) for a, b in zip(one, two))
            put(16 * group + 8 + r, *(jnp.where(even_y, a, b) for a, b in pairs))
            put(16 * group + 14 + r, *(jnp.where(even_y, b, a) for a, b in pairs))


def sides_received(first, second):
    even = even_on("gx")
    return jnp.where(even, first, second), jnp.where(even, second, first)


def extended(tall, from_right, from_left, k, dry=False):
    lane = lanes_of((16, 128))
    side = jnp.where(
        lane < 64,
        pltpu.roll(from_right, (128 - 2 * k) % 128, 1),
        pltpu.roll(from_left, 126 - 2 * k, 1),
    )
    if dry:
        side = jnp.where((lane < 2) | (lane >= 126), side, 0.0)
    return jnp.concatenate([tall, side], axis=1)


def beside(value):
    rows, cols = value.shape
    return (
        pltpu.roll(value, 1, 0),
        pltpu.roll(value, rows - 1, 0),
        pltpu.roll(value, 1, 1),
        pltpu.roll(value, cols - 1, 1),
    )


def spread(value, links):
    change = jnp.zeros_like(value)
    for link, near in zip(links, beside(value)):
        change = change + link * (near - value)
    return value + mixing_rate * change


def links_of(wet):
    return tuple(wet * near for near in beside(wet))


def shelf_melt(surface_temp, surface_salt, friction, pressure, wet_top):
    heat_gain = jnp.where(wet_top > 0, friction, 1.0)
    salt_safe = jnp.where(wet_top > 0, surface_salt, 34.0)
    salt_gain = heat_gain / salt_ratio
    curvature = heat_gain * liquidus_slope
    linear = (
        heat_gain * (surface_temp - liquidus_base - liquidus_depth * pressure)
        + latent_ratio * salt_gain
    )
    constant = latent_ratio * salt_gain * salt_safe
    boundary_salt = (
        2.0 * constant / (linear + jnp.sqrt(linear * linear - 4.0 * curvature * constant))
    )
    boundary_temp = liquidus_slope * boundary_salt + liquidus_base + liquidus_depth * pressure
    heat_flux = heat_gain * (surface_temp - boundary_temp) * wet_top
    salt_flux = salt_gain * (salt_safe - boundary_salt) * wet_top
    return heat_flux, salt_flux, boundary_temp * wet_top


def centre_of(value):
    return value[0:8, 0:128]


def surface_body(
    tall, cols_first, cols_second, slot_row, slot_lane, slot_weight, slot_target, send, held, sems
):
    from_right, from_left = sides_received(cols_first[...], cols_second[...])

    def plane(p):
        group, k = (p // few, p % few) if p < 3 * few else (3, p - 3 * few)
        rows = slice(16 * group, 16 * group + 16)
        return extended(tall[p], from_right[rows], from_left[rows], k, group == 2)

    planes = [plane(p) for p in range(12)]
    wets = planes[2 * few : 3 * few]
    mixing, rub, press = planes[9:12]
    first = mixing * (wets[0] * wets[1])
    second = mixing * (wets[1] * wets[2])
    links = [links_of(value) for value in wets]
    stepped = []
    for field in range(2):
        near = [spread(planes[few * field + k], links[k]) for k in range(few)]
        flux = first * (near[1] - near[0])
        under = second * (near[2] - near[1])
        stepped.append((near[0] + flux, near[1] + under - flux))
    heat, brine, base_one = shelf_melt(stepped[0][0], stepped[1][0], rub, press, wets[0])
    tops = (stepped[0][0] - relax_rate * heat, stepped[1][0] - relax_rate * brine)
    later = []
    for field in range(2):
        near0 = spread(tops[field], links[0])
        near1 = spread(stepped[field][1], links[1])
        later.append(centre_of(near0 + first * (near1 - near0)))
    heat_two, _, base_two = shelf_melt(
        later[0], later[1], centre_of(rub), centre_of(press), centre_of(wets[0])
    )
    melt = 0.5 * (centre_of(heat) / latent_ratio + heat_two / latent_ratio)
    base = 0.5 * (centre_of(base_one) + base_two)

    melts = [jnp.broadcast_to(melt[r : r + 1, :], (8, 128)) for r in range(8)]
    bases = [jnp.broadcast_to(base[r : r + 1, :], (8, 128)) for r in range(8)]

    def leave(i):
        rows = pl.ds(pl.multiple_of(chunk * batch * i, 8), chunk * batch)
        return pltpu.make_async_copy(held.at[rows], send.at[rows], sems.at[i])

    def owners(i, carry):
        out = held.at[pl.ds(pl.multiple_of(chunk * batch * i, 8), chunk * batch)]
        targets = slot_target[pl.ds(pl.multiple_of(batch * i, 8), batch), :]
        for j in range(batch):
            at = pl.ds(pl.multiple_of(8 * batch * i + 8 * j, 8), 8)
            lane = slot_lane[at, :]
            row = slot_row[at, :]
            weight = slot_weight[at, :]
            melt_here = jnp.take_along_axis(melts[0], lane, axis=1)
            base_here = jnp.take_along_axis(bases[0], lane, axis=1)
            for r in range(1, 8):
                hit = row == r
                melt_here = jnp.where(
                    hit, jnp.take_along_axis(melts[r], lane, axis=1), melt_here
                )
                base_here = jnp.where(
                    hit, jnp.take_along_axis(bases[r], lane, axis=1), base_here
                )
            out[chunk * j : chunk * j + 8, :] = weight * melt_here
            out[chunk * j + 8 : chunk * j + 16, :] = weight * base_here
            out[chunk * j + 16 : chunk * j + 24, :] = weight
            out[chunk * j + 24 : chunk * j + 25, :] = targets[j : j + 1, :]
        leave(i).start()
        return carry

    count = slot_target.shape[0] // batch
    lax.fori_loop(0, count, owners, 0)
    for i in range(count):
        leave(i).wait()


def slot_body(
    owner,
    target,
    column,
    weight,
    centre,
    slot_row,
    slot_lane,
    slot_weight,
    slot_target,
    low_side,
    high_side,
):
    own_columns(centre, low_side, high_side)
    count = owner.shape[1]
    tiles = count // 128
    row = lax.broadcasted_iota(jnp.int32, (128, 128), 0)
    col = lax.broadcasted_iota(jnp.int32, (128, 128), 1)

    def as_rows(value):
        return [
            jnp.sum(
                jnp.where(row == col, value[:, 128 * t : 128 * t + 128], 0), axis=1, keepdims=True
            )
            for t in range(tiles)
        ]

    owner_lane = owner[...]
    owner_row = as_rows(owner_lane)
    ranks = []
    for t in range(tiles):
        here = owner_lane[:, 128 * t : 128 * t + 128]
        seen = jnp.where((owner_row[t] == here) & (row < col), 1, 0)
        for before in range(t):
            seen = seen + jnp.where(owner_row[before] == here, 1, 0)
        ranks.append(jnp.sum(seen, axis=0, keepdims=True))
    rank_lane = jnp.concatenate(ranks, axis=1)
    rank_row = jnp.concatenate(as_rows(rank_lane), axis=0)
    target_row = jnp.concatenate(as_rows(target[...]), axis=0)
    slot = owner_lane * slots + rank_lane
    total = slot_row.shape[0]
    pick = jnp.where(lax.broadcasted_iota(jnp.int32, (total, count), 0) == slot, 1.0, 0.0)
    value = weight[...]
    high = value.astype(bf16)
    low = (value - high.astype(f32)).astype(bf16)
    places = column[...]
    table = jnp.concatenate(
        [
            high,
            low,
            (places >> 7).astype(f32).astype(bf16),
            (places & 127).astype(f32).astype(bf16),
        ],
        axis=1,
    )
    sorted_ = jnp.dot(pick.astype(bf16), table, preferred_element_type=f32)
    slot_weight[...] = sorted_[:, 0:128] + sorted_[:, 128:256]
    slot_row[...] = sorted_[:, 256:384].astype(jnp.int32)
    slot_lane[...] = sorted_[:, 384:512].astype(jnp.int32)
    lane = lax.broadcasted_iota(jnp.int32, (count, 128), 1)
    spot = jnp.where(rank_row == lane % slots, target_row, 0).astype(f32).astype(bf16)
    holds = jnp.where(lax.broadcasted_iota(jnp.int32, (128, count), 0) == owner_lane, 1.0, 0.0)
    slot_target[...] = jnp.dot(holds.astype(bf16), spot, preferred_element_type=f32)


def ocean_body(
    centre,
    rows_first,
    rows_second,
    cols_first,
    cols_second,
    new_temp,
    new_salt,
    near,
    wets,
    middle_links,
    later,
    from_right,
    from_left,
    tall,
):
    for at in range(3 * levels + 3):
        tall_plane(tall, at, centre[at], rows_first, rows_second, at)
    from_right[...], from_left[...] = sides_received(cols_first[...], cols_second[...])
    for end in (0, levels + 1):
        wets[end] = jnp.zeros((16, 256), f32)
        for field in range(2):
            near[field, end] = jnp.zeros((16, 256), f32)
            later[field, end] = jnp.zeros((8, 128), f32)
    mixing, rub, press = (
        extended(tall[3 * levels + p], from_right[48:64, :], from_left[48:64, :], p)
        for p in range(3)
    )

    def group_of(ref, group):
        return ref[16 * group : 16 * group + 16, :]

    def extend(group, k):
        return extended(
            tall[group * levels + k],
            group_of(from_right, group),
            group_of(from_left, group),
            k,
            group == 2,
        )

    unroll = 4

    def spread_level(k):
        water = extend(2, k)
        links = links_of(water)
        wets[k + 1] = water
        for place, link in enumerate(links):
            middle_links[k, place] = centre_of(link)
        for field in range(2):
            near[field, k + 1] = spread(extend(field, k), links)

    def mix_level(k, top):
        water = wets[k + 1]
        under = mixing * (water * wets[k + 2])
        over = mixing * (wets[k] * water)
        once = []
        for field in range(2):
            value = near[field, k + 1]
            value_under = under * (near[field, k + 2] - value)
            value_over = over * (value - near[field, k])
            once.append(value + value_under - value_over)
        if top:
            heat, brine, _ = shelf_melt(once[0], once[1], rub, press, water)
            once = [once[0] - relax_rate * heat, once[1] - relax_rate * brine]
        for field in range(2):
            change = jnp.zeros((8, 128), f32)
            middle = centre_of(once[field])
            for place, side in enumerate(beside(once[field])):
                change = change + middle_links[k, place] * (centre_of(side) - middle)
            later[field, k + 1] = middle + mixing_rate * change

    def finish_level(k, top):
        water = centre_of(wets[k + 1])
        mixing_c = centre_of(mixing)
        under = mixing_c * (water * centre_of(wets[k + 2]))
        over = mixing_c * (centre_of(wets[k]) * water)
        done = []
        for field in range(2):
            value = later[field, k + 1]
            value_under = under * (later[field, k + 2] - value)
            value_over = over * (value - later[field, k])
            done.append(value + value_under - value_over)
        if top:
            heat, brine, _ = shelf_melt(done[0], done[1], centre_of(rub), centre_of(press), water)
            done = [done[0] - relax_rate * heat, done[1] - relax_rate * brine]
        new_temp[k] = done[0]
        new_salt[k] = done[1]

    def every(step):
        def several(i, carry):
            for j in range(unroll):
                step(unroll * i + j)
            return carry

        lax.fori_loop(0, levels // unroll, several, 0)

    every(spread_level)
    every(lambda k: mix_level(k, False))
    mix_level(0, True)
    every(lambda k: finish_level(k, False))
    finish_level(0, True)


def column_body(
    enthalpy, surface, transition, area, offset, factor, pivot_end, side_end, per_area
):
    per_area[...] = 1.0 / area[...]
    count = enthalpy.shape[0]
    side = enthalpy[...].reshape(count, 32, 128)
    change_at = transition[...]
    rates = [jnp.where(k < change_at, cold_rate, temperate_rate) for k in range(count)]
    inner = [0.5 * (rates[k] + rates[k + 1]) for k in range(count - 1)]
    ratios = []
    values = []
    for k in range(count - 1):
        if k == 0:
            pivot = 1.0 + rates[0] + inner[0]
            right = side[0] + rates[0] * surface[...]
        else:
            pivot = 1.0 + inner[k - 1] + inner[k] + inner[k - 1] * ratios[-1]
            right = side[k] + inner[k - 1] * values[-1]
        scale = 1.0 / pivot
        ratios.append(-inner[k] * scale)
        values.append(right * scale)
    pivot_end[...] = 1.0 + inner[-1] + inner[-1] * ratios[-1]
    side_end[...] = side[count - 1] + inner[-1] * values[-1]
    offsets = [jnp.zeros((32, 128), f32)]
    factors = [jnp.ones((32, 128), f32)]
    for k in range(count - 2, -1, -1):
        offsets.append(values[k] - ratios[k] * offsets[-1])
        factors.append(-ratios[k] * factors[-1])
    offset[...] = jnp.stack(offsets[::-1]).reshape(count, 4096)
    factor[...] = jnp.stack(factors[::-1]).reshape(count, 4096)


def collect_body(
    got,
    offset,
    factor,
    pivot_end,
    side_end,
    per_area,
    new_enthalpy,
    melt,
    held,
    held_melt,
    sems,
):
    sums = jnp.zeros((32, 384), f32)
    lane = lax.broadcasted_iota(jnp.int32, (1, 128), 1) // slots
    wanted = lax.broadcasted_iota(jnp.int32, (32, 128), 0).astype(f32)
    for group in range(8):
        parts = ([], [], [])
        target = jnp.zeros((1, 128), f32)
        for s in range(16):
            at = chunk * (16 * group + s)
            for place in range(3):
                parts[place].append(got[at + 8 * place : at + 8 * place + 8, :])
            target = jnp.where(lane == s, got[at + 24 : at + 25, :], target)
        hot = jnp.where(wanted == target, 1.0, 0.0).astype(bf16)
        value = jnp.concatenate([jnp.concatenate(p, axis=0) for p in parts], axis=1)
        high = value.astype(bf16)
        low = (value - high.astype(f32)).astype(bf16)
        for piece in (high, low):
            sums = sums + jnp.dot(hot, piece, preferred_element_type=f32)
    scale = per_area[...]
    held_melt[...] = sums[:, 0:128] * scale
    copies = [pltpu.make_async_copy(held_melt, melt, sems.at[0])]
    copies[0].start()
    base_sum = sums[:, 128:256] * scale
    cover_sum = sums[:, 256:384] * scale
    last = (side_end[...] + base_sum) / (pivot_end[...] + cover_sum)
    last = last.reshape(1, 4096)
    for k in range(0, held.shape[0], 8):
        rows = pl.ds(k, 8)
        held[rows, :] = offset[rows, :] + factor[rows, :] * last
        copy = pltpu.make_async_copy(held.at[rows], new_enthalpy.at[rows], sems.at[1 + k // 8])
        copy.start()
        copies.append(copy)
    for copy in copies:
        copy.wait()


def local(
    ocean_temp,
    ocean_salt,
    wet_mask,
    vertical_mix,
    friction,
    pressure,
    pair_column,
    pair_weight,
    block_owner,
    block_target,
    enthalpy,
    surface_enthalpy,
    transition_layer,
    column_area,
):
    shape = jax.ShapeDtypeStruct
    ocean = (ocean_temp, ocean_salt, wet_mask, vertical_mix, friction, pressure)
    count_x = lax.axis_size("gx")
    count_y = lax.axis_size("gy")
    devices = count_x * count_y

    def chip(*dims, dtype=f32):
        return pltpu.VMEM(dims, dtype)

    def exchange(first, second, axis, count):
        pairs = [(i, i ^ 1) for i in range(count)]
        later = [(i + 1, (i ^ 1) + 1) for i in range(count - 2)]
        first = lax.ppermute(first, axis, pairs)
        return first, lax.ppermute(second, axis, later)

    rows_first, rows_second, centre = call(
        all_rows_body,
        (chip(halo_rows, 128), chip(halo_rows, 128), chip(3 * levels + 3, 8, 128)),
        ocean,
        cost=(10**5, 10**6),
    )
    rows_first, rows_second = exchange(rows_first, rows_second, "gy", count_y)
    slot_row, slot_lane, slot_weight, slot_target, low_side, high_side = call(
        slot_body,
        (
            chip(devices * slots, 128, dtype=jnp.int32),
            chip(devices * slots, 128, dtype=jnp.int32),
            chip(devices * slots, 128),
            chip(devices, 128),
            chip(32, 128),
            chip(32, 128),
        ),
        (
            block_owner.reshape(1, -1),
            block_target.reshape(1, -1),
            pair_column,
            pair_weight,
            Near(centre),
        ),
        cost=(2 * 10**9, 3 * 10**6),
    )
    rows_first, slot_target = lax.optimization_barrier((rows_first, slot_target))
    cols_first, cols_second, tall = call(
        all_cols_body,
        (chip(64, 128), chip(64, 128), chip(12, 16, 128)),
        tuple(Near(a) for a in (centre, low_side, high_side, rows_first, rows_second)),
        cost=(10**5, 10**6),
    )
    cols_first, cols_second = exchange(cols_first, cols_second, "gx", count_x)
    send = call(
        surface_body,
        shape((devices * chunk, 128), f32),
        tuple(
            Near(a)
            for a in (
                tall,
                cols_first,
                cols_second,
                slot_row,
                slot_lane,
                slot_weight,
                slot_target,
            )
        ),
        [pltpu.VMEM((devices * chunk, 128), f32), pltpu.SemaphoreType.DMA((devices // batch,))],
        cost=(10**6, 3 * 10**6),
        own_copies=True,
    )
    send, cols_first, surface_enthalpy = lax.optimization_barrier(
        (send, cols_first, surface_enthalpy)
    )
    got = lax.all_to_all(
        send.reshape(devices, chunk, 1, 128),
        ("gx", "gy"),
        split_axis=0,
        concat_axis=0,
        tiled=True,
    ).reshape(devices * chunk, 128)
    new_temp, new_salt = call(
        ocean_body,
        (shape(ocean_temp.shape, f32), shape(ocean_salt.shape, f32)),
        tuple(Near(a) for a in (centre, rows_first, rows_second, cols_first, cols_second)),
        [
            pltpu.VMEM((2, levels + 2, 16, 256), f32),
            pltpu.VMEM((levels + 2, 16, 256), f32),
            pltpu.VMEM((levels, 4, 8, 128), f32),
            pltpu.VMEM((2, levels + 2, 8, 128), f32),
            pltpu.VMEM((64, 128), f32),
            pltpu.VMEM((64, 128), f32),
            pltpu.VMEM((3 * levels + 3, 16, 128), f32),
        ],
        cost=(10**8, 2 * 10**6),
    )
    new_temp, surface_enthalpy = lax.optimization_barrier((new_temp, surface_enthalpy))
    offset, factor, pivot_end, side_end, per_area = call(
        column_body,
        (chip(*enthalpy.shape), chip(*enthalpy.shape)) + (chip(32, 128),) * 3,
        (
            enthalpy,
            surface_enthalpy.reshape(32, 128),
            transition_layer.reshape(32, 128),
            column_area.reshape(32, 128),
        ),
        cost=(10**8, 2 * 10**6),
    )
    new_enthalpy, melt = call(
        collect_body,
        (shape(enthalpy.shape, f32), shape((32, 128), f32)),
        tuple(Near(a) for a in (got, offset, factor, pivot_end, side_end, per_area)),
        [
            pltpu.VMEM(enthalpy.shape, f32),
            pltpu.VMEM((32, 128), f32),
            pltpu.SemaphoreType.DMA((1 + enthalpy.shape[0] // 8,)),
        ],
        cost=(10**9, 4 * 10**6),
        own_copies=True,
    )
    return new_temp, new_salt, new_enthalpy, melt.reshape(-1)


def solution(mesh):
    return jax.shard_map(
        local,
        mesh=mesh,
        in_specs=(
            P(None, "gy", "gx"),
            P(None, "gy", "gx"),
            P(None, "gy", "gx"),
            P("gy", "gx"),
            P("gy", "gx"),
            P("gy", "gx"),
            P(("gx", "gy"), None),
            P(("gx", "gy"), None),
            P(("gx", "gy"), None),
            P(("gx", "gy")),
            P(None, ("gx", "gy")),
            P(("gx", "gy")),
            P(("gx", "gy")),
            P(("gx", "gy")),
        ),
        out_specs=(
            P(None, "gy", "gx"),
            P(None, "gy", "gx"),
            P(None, ("gx", "gy")),
            P(("gx", "gy")),
        ),
        check_vma=False,
    )
```

```python
import jax
import jax.numpy as jnp
from jax import lax
from jax.experimental import pallas as pl
from jax.experimental.pallas import tpu as pltpu
from jax.sharding import PartitionSpec as P


mixing_rate = 0.2
liquidus_slope = -0.0573
liquidus_base = 0.0832
liquidus_depth = -0.000753
latent_ratio = 4.0
salt_ratio = 35.0
relax_rate = 0.1
cold_rate = 2.0
temperate_rate = 0.2

f32 = jnp.float32
bf16 = jnp.bfloat16
levels = 64
slots = 8
chunk = 3 * slots + 1
halo_rows = 392
few = 3
batch = 64


def lanes_of(shape):
    return lax.broadcasted_iota(jnp.int32, shape, len(shape) - 1)


def call(body, outs, ins, scratch=(), cost=(0, 0), own_copies=False):
    arrays, specs = [], []
    for item in ins:
        if isinstance(item, Near):
            arrays.append(pltpu.with_memory_space_constraint(item.array, pltpu.VMEM))
            specs.append(pl.BlockSpec(memory_space=pltpu.VMEM))
        else:
            array, block, index = item if isinstance(item, tuple) else (item, item.shape, None)
            arrays.append(pltpu.with_memory_space_constraint(array, pltpu.HBM))
            specs.append(part(block, index or (0,) * len(block)))
    if own_copies:
        out_specs = jax.tree.map(lambda o: pl.BlockSpec(memory_space=pltpu.HBM), outs)
    else:
        out_specs = jax.tree.map(
            lambda o: part(o.shape, (0,) * len(o.shape))
            if isinstance(o, jax.ShapeDtypeStruct)
            else pl.BlockSpec(memory_space=pltpu.VMEM),
            outs,
        )
    return pl.pallas_call(
        body,
        out_shape=outs,
        grid=(1,),
        in_specs=specs,
        out_specs=out_specs,
        scratch_shapes=scratch,
        compiler_params=pltpu.CompilerParams(vmem_limit_bytes=16 << 20),
        cost_estimate=pl.CostEstimate(flops=cost[0], bytes_accessed=cost[1], transcendentals=0),
    )(*arrays)


class Near:
    def __init__(self, array):
        self.array = array


def part(shape, index):
    return pl.BlockSpec(tuple(shape), lambda i: tuple(index))


def even_on(axis):
    return lax.axis_index(axis) % 2 == 0


def all_rows_body(temp, salt, wet, mix, friction, pressure, first, second, centre):
    even = even_on("gy")

    def put(at, high, low):
        first[at : at + 2, :] = jnp.where(even, high, low)
        second[at : at + 2, :] = jnp.where(even, low, high)

    at = 0
    for source in (temp, salt, wet):
        for k in range(levels):
            value = source[k].astype(f32)
            centre[at // 2] = value
            put(at, value[6:8, :], value[0:2, :])
            at += 2
    for source in (mix, friction, pressure):
        centre[at // 2] = source[...]
        put(at, source[6:8, :], source[0:2, :])
        at += 2
    put(at, jnp.zeros((2, 128), f32), jnp.zeros((2, 128), f32))


def tall_plane(tall, at, value, rows_first, rows_second, place):
    at_first = jnp.where(even_on("gy"), 8, 14)
    at_second = 22 - at_first
    tall[at, 0:8, :] = value
    tall[at, 8:16, :] = jnp.zeros((8, 128), f32)
    tall[at, pl.ds(at_first, 2), :] = rows_first[2 * place : 2 * place + 2, :]
    tall[at, pl.ds(at_second, 2), :] = rows_second[2 * place : 2 * place + 2, :]


plane_groups = (levels, levels, levels, 3)


def own_columns(centre, low_side, high_side):
    half = lanes_of((8, 128)) // 2
    start = 0
    for group, count in enumerate(plane_groups):
        low = jnp.zeros((8, 128), f32)
        high = jnp.zeros((8, 128), f32)
        for k in range(count):
            value = centre[start + k]
            here = half == k
            low = jnp.where(here, pltpu.roll(value, 2 * k, 1), low)
            high = jnp.where(here, pltpu.roll(value, (2 * k + 2) % 128, 1), high)
        low_side[8 * group : 8 * group + 8, :] = low
        high_side[8 * group : 8 * group + 8, :] = high
        start += count


def all_cols_body(
    centre, low_side, high_side, rows_first, rows_second, first, second, tall
):
    places = [field * levels + k for field in range(3) for k in range(few)]
    places += [3 * levels + p for p in range(3)]
    for at, place in enumerate(places):
        tall_plane(tall, at, centre[place], rows_first, rows_second, place)

    even_x = even_on("gx")
    even_y = even_on("gy")
    lane = lanes_of((8, 128))
    row = lax.broadcasted_iota(jnp.int32, (8, 128), 0)
    ahead = ((lane - row % 2) & 127) // 2 - row // 2

    def put(at, low, high):
        first[at : at + low.shape[0], :] = jnp.where(even_x, high, low)
        second[at : at + low.shape[0], :] = jnp.where(even_x, low, high)

    def row_columns(rows, start, count):
        low = jnp.zeros((8, 128), f32)
        high = jnp.zeros((8, 128), f32)
        for k in range(0, count, 4):
            value = rows[start + 2 * k : start + 2 * k + 8, :]
            here = ahead == k
            turned = pltpu.roll(value, 2 * k, 1, stride=1, stride_axis=0)
            low = jnp.where(here, turned, low)
            if 2 * k + 2 + 7 < 128:
                turned = pltpu.roll(value, 2 * k + 2, 1, stride=1, stride_axis=0)
            else:
                turned = pltpu.roll(turned, 2, 1)
            high = jnp.where(here, turned, high)
        return tuple(
            (
                jnp.sum(jnp.where(row % 2 == 0, value, 0.0), axis=0, keepdims=True),
                pltpu.roll(
                    jnp.sum(jnp.where(row % 2 == 1, value, 0.0), axis=0, keepdims=True), 127, 1
                ),
            )
            for value in (low, high)
        )

    for group in range(4):
        own = slice(8 * group, 8 * group + 8)
        put(16 * group, low_side[own, :], high_side[own, :])
        put(16 * group + 8, jnp.zeros((8, 128), f32), jnp.zeros((8, 128), f32))
        padded = levels if group < 3 else 4
        one = row_columns(rows_first, 2 * group * levels, padded)
        two = row_columns(rows_second, 2 * group * levels, padded)
        for r in range(2):
            pairs = tuple((a[r], b[r]) for a, b in zip(one, two))
            put(16 * group + 8 + r, *(jnp.where(even_y, a, b) for a, b in pairs))
            put(16 * group + 14 + r, *(jnp.where(even_y, b, a) for a, b in pairs))


def sides_received(first, second):
    even = even_on("gx")
    return jnp.where(even, first, second), jnp.where(even, second, first)


def extended(tall, from_right, from_left, k, dry=False):
    lane = lanes_of((16, 128))
    side = jnp.where(
        lane < 64,
        pltpu.roll(from_right, (128 - 2 * k) % 128, 1),
        pltpu.roll(from_left, 126 - 2 * k, 1),
    )
    if dry:
        side = jnp.where((lane < 2) | (lane >= 126), side, 0.0)
    return jnp.concatenate([tall, side], axis=1)


def beside(value):
    rows, cols = value.shape
    return (
        pltpu.roll(value, 1, 0),
        pltpu.roll(value, rows - 1, 0),
        pltpu.roll(value, 1, 1),
        pltpu.roll(value, cols - 1, 1),
    )


def spread(value, links):
    change = jnp.zeros_like(value)
    for link, near in zip(links, beside(value)):
        change = change + link * (near - value)
    return value + mixing_rate * change


def links_of(wet):
    return tuple(wet * near for near in beside(wet))


def shelf_melt(surface_temp, surface_salt, friction, pressure, wet_top):
    heat_gain = jnp.where(wet_top > 0, friction, 1.0)
    salt_safe = jnp.where(wet_top > 0, surface_salt, 34.0)
    salt_gain = heat_gain / salt_ratio
    curvature = heat_gain * liquidus_slope
    linear = (
        heat_gain * (surface_temp - liquidus_base - liquidus_depth * pressure)
        + latent_ratio * salt_gain
    )
    constant = latent_ratio * salt_gain * salt_safe
    boundary_salt = (
        2.0 * constant / (linear + jnp.sqrt(linear * linear - 4.0 * curvature * constant))
    )
    boundary_temp = liquidus_slope * boundary_salt + liquidus_base + liquidus_depth * pressure
    heat_flux = heat_gain * (surface_temp - boundary_temp) * wet_top
    salt_flux = salt_gain * (salt_safe - boundary_salt) * wet_top
    return heat_flux, salt_flux, boundary_temp * wet_top


def centre_of(value):
    return value[0:8, 0:128]


def surface_body(
    tall,
    cols_first,
    cols_second,
    column,
    weight,
    slot_pick,
    slot_weight,
    slot_target,
    send,
    held,
    values,
    sems,
):
    from_right, from_left = sides_received(cols_first[...], cols_second[...])

    def plane(p):
        group, k = (p // few, p % few) if p < 3 * few else (3, p - 3 * few)
        rows = slice(16 * group, 16 * group + 16)
        return extended(tall[p], from_right[rows], from_left[rows], k, group == 2)

    planes = [plane(p) for p in range(12)]
    wets = planes[2 * few : 3 * few]
    mixing, rub, press = planes[9:12]
    first = mixing * (wets[0] * wets[1])
    second = mixing * (wets[1] * wets[2])
    links = [links_of(value) for value in wets]
    stepped = []
    for field in range(2):
        near = [spread(planes[few * field + k], links[k]) for k in range(few)]
        flux = first * (near[1] - near[0])
        under = second * (near[2] - near[1])
        stepped.append((near[0] + flux, near[1] + under - flux))
    heat, brine, base_one = shelf_melt(stepped[0][0], stepped[1][0], rub, press, wets[0])
    tops = (stepped[0][0] - relax_rate * heat, stepped[1][0] - relax_rate * brine)
    later = []
    for field in range(2):
        near0 = spread(tops[field], links[0])
        near1 = spread(stepped[field][1], links[1])
        later.append(centre_of(near0 + first * (near1 - near0)))
    heat_two, _, base_two = shelf_melt(
        later[0], later[1], centre_of(rub), centre_of(press), centre_of(wets[0])
    )
    melt = 0.5 * (centre_of(heat) / latent_ratio + heat_two / latent_ratio)
    base = 0.5 * (centre_of(base_one) + base_two)

    melts = [jnp.broadcast_to(melt[r : r + 1, :], (8, 128)) for r in range(8)]
    bases = [jnp.broadcast_to(base[r : r + 1, :], (8, 128)) for r in range(8)]

    def blocks(i, carry):
        for j in range(4):
            at = pl.ds(pl.multiple_of(64 * i + 16 * j, 16), 16)
            found = []
            for half in range(2):
                here = pl.ds(pl.multiple_of(64 * i + 16 * j + 8 * half, 8), 8)
                places = column[here, :]
                lane = places & 127
                row = places >> 7
                melt_here = jnp.take_along_axis(melts[0], lane, axis=1)
                base_here = jnp.take_along_axis(bases[0], lane, axis=1)
                for r in range(1, 8):
                    hit = row == r
                    melt_here = jnp.where(
                        hit, jnp.take_along_axis(melts[r], lane, axis=1), melt_here
                    )
                    base_here = jnp.where(
                        hit, jnp.take_along_axis(bases[r], lane, axis=1), base_here
                    )
                found.append((weight[here, :] * melt_here, weight[here, :] * base_here))
            for place in range(2):
                both = jnp.concatenate([found[0][place], found[1][place]], axis=0)
                values[at, 256 * place : 256 * place + 256] = two_pieces(both)
        return carry

    lax.fori_loop(0, column.shape[0] // 64, blocks, 0)

    count = slot_target.shape[0] // batch
    copies = []
    for i in range(count):
        first = batch * i
        rows = slice(slots * first, slots * (first + batch))
        placed = jnp.dot(slot_pick[rows, :], values[...], preferred_element_type=f32)
        melt_here = placed[:, 0:128] + placed[:, 128:256]
        base_here = placed[:, 256:384] + placed[:, 384:512]
        for j in range(batch):
            at = chunk * (first + j)
            own = slice(slots * j, slots * j + slots)
            held[at : at + 8, :] = melt_here[own, :]
            held[at + 8 : at + 16, :] = base_here[own, :]
            slot = slots * (first + j)
            held[at + 16 : at + 24, :] = slot_weight[slot : slot + slots, :]
            held[at + 24 : at + 25, :] = slot_target[first + j : first + j + 1, :]
        leaving = pl.ds(chunk * first, chunk * batch)
        copy = pltpu.make_async_copy(held.at[leaving], send.at[leaving], sems.at[i])
        copy.start()
        copies.append(copy)
    for copy in copies:
        copy.wait()


def two_pieces(value):
    high = value.astype(bf16)
    return jnp.concatenate([high, (value - high.astype(f32)).astype(bf16)], axis=1)


def slot_body(
    owner,
    target,
    weight,
    centre,
    slot_pick,
    slot_weight,
    slot_target,
    low_side,
    high_side,
):
    own_columns(centre, low_side, high_side)
    count = owner.shape[1]
    tiles = count // 128
    row = lax.broadcasted_iota(jnp.int32, (128, 128), 0)
    col = lax.broadcasted_iota(jnp.int32, (128, 128), 1)

    def as_rows(value):
        return [
            jnp.sum(
                jnp.where(row == col, value[:, 128 * t : 128 * t + 128], 0), axis=1, keepdims=True
            )
            for t in range(tiles)
        ]

    owner_lane = owner[...]
    owner_row = as_rows(owner_lane)
    ranks = []
    for t in range(tiles):
        here = owner_lane[:, 128 * t : 128 * t + 128]
        seen = jnp.where((owner_row[t] == here) & (row < col), 1, 0)
        for before in range(t):
            seen = seen + jnp.where(owner_row[before] == here, 1, 0)
        ranks.append(jnp.sum(seen, axis=0, keepdims=True))
    rank_lane = jnp.concatenate(ranks, axis=1)
    rank_row = jnp.concatenate(as_rows(rank_lane), axis=0)
    target_row = jnp.concatenate(as_rows(target[...]), axis=0)
    slot = owner_lane * slots + rank_lane
    total = slot_weight.shape[0]
    pick = jnp.where(lax.broadcasted_iota(jnp.int32, (total, count), 0) == slot, 1.0, 0.0)
    slot_pick[...] = pick.astype(bf16)
    sorted_ = jnp.dot(slot_pick[...], two_pieces(weight[...]), preferred_element_type=f32)
    slot_weight[...] = sorted_[:, 0:128] + sorted_[:, 128:256]
    lane = lax.broadcasted_iota(jnp.int32, (count, 128), 1)
    spot = jnp.where(rank_row == lane % slots, target_row, 0).astype(f32).astype(bf16)
    holds = jnp.where(lax.broadcasted_iota(jnp.int32, (128, count), 0) == owner_lane, 1.0, 0.0)
    slot_target[...] = jnp.dot(holds.astype(bf16), spot, preferred_element_type=f32)


def ocean_body(
    centre,
    rows_first,
    rows_second,
    cols_first,
    cols_second,
    new_temp,
    new_salt,
    near,
    wets,
    middle_links,
    later,
    from_right,
    from_left,
    tall,
):
    for at in range(3 * levels + 3):
        tall_plane(tall, at, centre[at], rows_first, rows_second, at)
    from_right[...], from_left[...] = sides_received(cols_first[...], cols_second[...])
    for end in (0, levels + 1):
        wets[end] = jnp.zeros((16, 256), f32)
        for field in range(2):
            near[field, end] = jnp.zeros((16, 256), f32)
            later[field, end] = jnp.zeros((8, 128), f32)
    mixing, rub, press = (
        extended(tall[3 * levels + p], from_right[48:64, :], from_left[48:64, :], p)
        for p in range(3)
    )

    def group_of(ref, group):
        return ref[16 * group : 16 * group + 16, :]

    def extend(group, k):
        return extended(
            tall[group * levels + k],
            group_of(from_right, group),
            group_of(from_left, group),
            k,
            group == 2,
        )

    unroll = 4

    def spread_level(k):
        water = extend(2, k)
        links = links_of(water)
        wets[k + 1] = water
        for place, link in enumerate(links):
            middle_links[k, place] = centre_of(link)
        for field in range(2):
            near[field, k + 1] = spread(extend(field, k), links)

    def mix_level(k, top):
        water = wets[k + 1]
        under = mixing * (water * wets[k + 2])
        over = mixing * (wets[k] * water)
        once = []
        for field in range(2):
            value = near[field, k + 1]
            value_under = under * (near[field, k + 2] - value)
            value_over = over * (value - near[field, k])
            once.append(value + value_under - value_over)
        if top:
            heat, brine, _ = shelf_melt(once[0], once[1], rub, press, water)
            once = [once[0] - relax_rate * heat, once[1] - relax_rate * brine]
        for field in range(2):
            change = jnp.zeros((8, 128), f32)
            middle = centre_of(once[field])
            for place, side in enumerate(beside(once[field])):
                change = change + middle_links[k, place] * (centre_of(side) - middle)
            later[field, k + 1] = middle + mixing_rate * change

    def finish_level(k, top):
        water = centre_of(wets[k + 1])
        mixing_c = centre_of(mixing)
        under = mixing_c * (water * centre_of(wets[k + 2]))
        over = mixing_c * (centre_of(wets[k]) * water)
        done = []
        for field in range(2):
            value = later[field, k + 1]
            value_under = under * (later[field, k + 2] - value)
            value_over = over * (value - later[field, k])
            done.append(value + value_under - value_over)
        if top:
            heat, brine, _ = shelf_melt(done[0], done[1], centre_of(rub), centre_of(press), water)
            done = [done[0] - relax_rate * heat, done[1] - relax_rate * brine]
        new_temp[k] = done[0]
        new_salt[k] = done[1]

    def every(step):
        def several(i, carry):
            for j in range(unroll):
                step(unroll * i + j)
            return carry

        lax.fori_loop(0, levels // unroll, several, 0)

    every(spread_level)
    every(lambda k: mix_level(k, False))
    mix_level(0, True)
    every(lambda k: finish_level(k, False))
    finish_level(0, True)


def column_body(
    enthalpy, surface, transition, area, offset, factor, pivot_end, side_end, per_area
):
    per_area[...] = 1.0 / area[...]
    count = enthalpy.shape[0]
    side = enthalpy[...].reshape(count, 32, 128)
    change_at = transition[...]
    rates = [jnp.where(k < change_at, cold_rate, temperate_rate) for k in range(count)]
    inner = [0.5 * (rates[k] + rates[k + 1]) for k in range(count - 1)]
    ratios = []
    values = []
    for k in range(count - 1):
        if k == 0:
            pivot = 1.0 + rates[0] + inner[0]
            right = side[0] + rates[0] * surface[...]
        else:
            pivot = 1.0 + inner[k - 1] + inner[k] + inner[k - 1] * ratios[-1]
            right = side[k] + inner[k - 1] * values[-1]
        scale = 1.0 / pivot
        ratios.append(-inner[k] * scale)
        values.append(right * scale)
    pivot_end[...] = 1.0 + inner[-1] + inner[-1] * ratios[-1]
    side_end[...] = side[count - 1] + inner[-1] * values[-1]
    offsets = [jnp.zeros((32, 128), f32)]
    factors = [jnp.ones((32, 128), f32)]
    for k in range(count - 2, -1, -1):
        offsets.append(values[k] - ratios[k] * offsets[-1])
        factors.append(-ratios[k] * factors[-1])
    offset[...] = jnp.stack(offsets[::-1]).reshape(count, 4096)
    factor[...] = jnp.stack(factors[::-1]).reshape(count, 4096)


def collect_body(
    got,
    offset,
    factor,
    pivot_end,
    side_end,
    per_area,
    new_enthalpy,
    melt,
    held,
    held_melt,
    sems,
):
    sums = jnp.zeros((32, 384), f32)
    lane = lax.broadcasted_iota(jnp.int32, (1, 128), 1) // slots
    wanted = lax.broadcasted_iota(jnp.int32, (32, 128), 0).astype(f32)
    for group in range(8):
        parts = ([], [], [])
        target = jnp.zeros((1, 128), f32)
        for s in range(16):
            at = chunk * (16 * group + s)
            for place in range(3):
                parts[place].append(got[at + 8 * place : at + 8 * place + 8, :])
            target = jnp.where(lane == s, got[at + 24 : at + 25, :], target)
        hot = jnp.where(wanted == target, 1.0, 0.0).astype(bf16)
        value = jnp.concatenate([jnp.concatenate(p, axis=0) for p in parts], axis=1)
        high = value.astype(bf16)
        low = (value - high.astype(f32)).astype(bf16)
        for piece in (high, low):
            sums = sums + jnp.dot(hot, piece, preferred_element_type=f32)
    scale = per_area[...]
    held_melt[...] = sums[:, 0:128] * scale
    copies = [pltpu.make_async_copy(held_melt, melt, sems.at[0])]
    copies[0].start()
    base_sum = sums[:, 128:256] * scale
    cover_sum = sums[:, 256:384] * scale
    last = (side_end[...] + base_sum) / (pivot_end[...] + cover_sum)
    last = last.reshape(1, 4096)
    for k in range(0, held.shape[0], 8):
        rows = pl.ds(k, 8)
        held[rows, :] = offset[rows, :] + factor[rows, :] * last
        copy = pltpu.make_async_copy(held.at[rows], new_enthalpy.at[rows], sems.at[1 + k // 8])
        copy.start()
        copies.append(copy)
    for copy in copies:
        copy.wait()


def local(
    ocean_temp,
    ocean_salt,
    wet_mask,
    vertical_mix,
    friction,
    pressure,
    pair_column,
    pair_weight,
    block_owner,
    block_target,
    enthalpy,
    surface_enthalpy,
    transition_layer,
    column_area,
):
    shape = jax.ShapeDtypeStruct
    ocean = (ocean_temp, ocean_salt, wet_mask, vertical_mix, friction, pressure)
    count_x = lax.axis_size("gx")
    count_y = lax.axis_size("gy")
    devices = count_x * count_y

    def chip(*dims, dtype=f32):
        return pltpu.VMEM(dims, dtype)

    def exchange(first, second, axis, count):
        pairs = [(i, i ^ 1) for i in range(count)]
        later = [(i + 1, (i ^ 1) + 1) for i in range(count - 2)]
        first = lax.ppermute(first, axis, pairs)
        return first, lax.ppermute(second, axis, later)

    rows_first, rows_second, centre = call(
        all_rows_body,
        (chip(halo_rows, 128), chip(halo_rows, 128), chip(3 * levels + 3, 8, 128)),
        ocean,
        cost=(10**5, 10**6),
    )
    rows_first, rows_second = exchange(rows_first, rows_second, "gy", count_y)
    slot_pick, slot_weight, slot_target, low_side, high_side = call(
        slot_body,
        (
            chip(devices * slots, pair_column.shape[0], dtype=bf16),
            chip(devices * slots, 128),
            chip(devices, 128),
            chip(32, 128),
            chip(32, 128),
        ),
        (
            block_owner.reshape(1, -1),
            block_target.reshape(1, -1),
            pair_weight,
            Near(centre),
        ),
        cost=(2 * 10**9, 3 * 10**6),
    )
    rows_first, slot_target = lax.optimization_barrier((rows_first, slot_target))
    cols_first, cols_second, tall = call(
        all_cols_body,
        (chip(64, 128), chip(64, 128), chip(12, 16, 128)),
        tuple(Near(a) for a in (centre, low_side, high_side, rows_first, rows_second)),
        cost=(10**5, 10**6),
    )
    cols_first, cols_second = exchange(cols_first, cols_second, "gx", count_x)
    send = call(
        surface_body,
        shape((devices * chunk, 128), f32),
        (Near(tall), Near(cols_first), Near(cols_second), Near(pair_column), Near(pair_weight))
        + (Near(slot_pick), Near(slot_weight), Near(slot_target)),
        [
            pltpu.VMEM((devices * chunk, 128), f32),
            pltpu.VMEM((pair_column.shape[0], 512), bf16),
            pltpu.SemaphoreType.DMA((devices // batch,)),
        ],
        cost=(10**6, 3 * 10**6),
        own_copies=True,
    )
    send, cols_first, surface_enthalpy = lax.optimization_barrier(
        (send, cols_first, surface_enthalpy)
    )
    got = lax.all_to_all(
        send.reshape(devices, chunk, 1, 128),
        ("gx", "gy"),
        split_axis=0,
        concat_axis=0,
        tiled=True,
    ).reshape(devices * chunk, 128)
    new_temp, new_salt = call(
        ocean_body,
        (shape(ocean_temp.shape, f32), shape(ocean_salt.shape, f32)),
        tuple(Near(a) for a in (centre, rows_first, rows_second, cols_first, cols_second)),
        [
            pltpu.VMEM((2, levels + 2, 16, 256), f32),
            pltpu.VMEM((levels + 2, 16, 256), f32),
            pltpu.VMEM((levels, 4, 8, 128), f32),
            pltpu.VMEM((2, levels + 2, 8, 128), f32),
            pltpu.VMEM((64, 128), f32),
            pltpu.VMEM((64, 128), f32),
            pltpu.VMEM((3 * levels + 3, 16, 128), f32),
        ],
        cost=(10**8, 2 * 10**6),
    )
    new_temp, surface_enthalpy = lax.optimization_barrier((new_temp, surface_enthalpy))
    offset, factor, pivot_end, side_end, per_area = call(
        column_body,
        (chip(*enthalpy.shape), chip(*enthalpy.shape)) + (chip(32, 128),) * 3,
        (
            enthalpy,
            surface_enthalpy.reshape(32, 128),
            transition_layer.reshape(32, 128),
            column_area.reshape(32, 128),
        ),
        cost=(10**8, 2 * 10**6),
    )
    new_enthalpy, melt = call(
        collect_body,
        (shape(enthalpy.shape, f32), shape((32, 128), f32)),
        tuple(Near(a) for a in (got, offset, factor, pivot_end, side_end, per_area)),
        [
            pltpu.VMEM(enthalpy.shape, f32),
            pltpu.VMEM((32, 128), f32),
            pltpu.SemaphoreType.DMA((1 + enthalpy.shape[0] // 8,)),
        ],
        cost=(10**9, 4 * 10**6),
        own_copies=True,
    )
    return new_temp, new_salt, new_enthalpy, melt.reshape(-1)


def solution(mesh):
    return jax.shard_map(
        local,
        mesh=mesh,
        in_specs=(
            P(None, "gy", "gx"),
            P(None, "gy", "gx"),
            P(None, "gy", "gx"),
            P("gy", "gx"),
            P("gy", "gx"),
            P("gy", "gx"),
            P(("gx", "gy"), None),
            P(("gx", "gy"), None),
            P(("gx", "gy"), None),
            P(("gx", "gy")),
            P(None, ("gx", "gy")),
            P(("gx", "gy")),
            P(("gx", "gy")),
            P(("gx", "gy")),
        ),
        out_specs=(
            P(None, "gy", "gx"),
            P(None, "gy", "gx"),
            P(None, ("gx", "gy")),
            P(("gx", "gy")),
        ),
        check_vma=False,
    )
```
